256 devices in a mesh: section: 2 (over z_hi), dp: 32 (over z_lo, y, core), mp: 4 (over x).
Axes of the slice: x: 4, y: 4, z: 8 (z_hi: 2, z_lo: 4; z = z_hi * 4 + z_lo), core: 2. Of those that a mesh axis runs over, the one named last changes fastest.
Arguments:
- embeds: bfloat16 [2, 6144, 4096], P('section', 'dp', 'mp'), may hold values from -6 to 6
- lengths: int32 [32, 32], replicated, may hold values from 1 to 6, 120 in all within a row
- owners: int32 [32, 32], replicated, may hold values from 0 to 31, each once within a row
- w_query: bfloat16 [2, 4096, 2048], P('section', None, 'mp'), may hold values from -0.09375 to 0.09375
- w_key: bfloat16 [2, 4096, 512], P('section', None, 'mp'), may hold values from -0.09375 to 0.09375
- w_value: bfloat16 [2, 4096, 512], P('section', None, 'mp'), may hold values from -0.09375 to 0.09375
- w_out: bfloat16 [2, 2048, 4096], P('section', 'mp'), may hold values from -0.125 to 0.125
- cycle_grad: bfloat16 [2, 6144, 4096], P('section', 'dp', 'mp'), may hold values from -0.75 to 0.75
Outputs:
- cycled: bfloat16 [2, 6144, 4096], P('section', 'dp', 'mp')
- embed_grad: bfloat16 [2, 6144, 4096], P('section', 'dp', 'mp')
- grad_query: float32 [2, 4096, 2048], P('section', 'dp', 'mp')
- grad_key: float32 [2, 4096, 512], P('section', 'dp', 'mp')
- grad_value: float32 [2, 4096, 512], P('section', 'dp', 'mp')
- grad_output: float32 [2, 4096, 2048], P('section', 'dp', 'mp')
The draws below stay inside these ranges and needn't reach their ends.
Inputs may be any that keep to these rules, and one draw needn't show every extreme that they name: `owners`: each row names every dp index once.
All inputs are finite; a program needn't handle non-finite values.
Results may differ from the reference program's by a relative error of at most 0.04.
Values may be sent and summed in bfloat16 or wider, within the bound.
No kernel may reach another device: no remote copies, remote signals or barrier semaphores. Data moves between devices by JAX's collectives and lax.ppermute only.
A program may use at most 128 MiB of HBM per device.

```python
import math
import jax
import jax.numpy as jnp
import numpy as np
from jax import lax

D = 4096
HEADS = 16
KV_HEADS = 4
HEAD_DIM = 128
SLOT = 6
ROWS = 192
TOKENS = 6144
N_DP = 32
N_MP = 4


def with_spikes(result, own_key, source, target, blocks, factor):
    def block_of(dim):
        return (jnp.arange(result.shape[dim]) // (result.shape[dim] // blocks)).reshape((-1,) + (1,) * (result.ndim - 1 - dim))

    one_side = jax.random.permutation(own_key, blocks)[block_of(target)]
    other_side = (block_of(target) + blocks // 2) % blocks
    return jnp.where((block_of(source) == one_side) | (block_of(source) == other_side), factor * result, result)


def shard_levels(rng, extent, split, low, largest):
    factor_of = 1.0
    for dim, parts in split:
        heights = jax.random.uniform(jax.random.fold_in(jax.random.fold_in(rng, 6), dim), (parts,), jnp.float32, low / len(split), largest / len(split))
        factor_of = factor_of * jnp.repeat(jnp.exp(heights), extent[dim] // parts).reshape((-1,) + (1,) * (len(extent) - 1 - dim))
    return factor_of


def profile(count, total, bound, skew):
    loads = [(1 << 20) // math.isqrt(rank ** skew) + 1 for rank in range(2, count + 1)]
    spare, given = total - bound - (count - 1), [1] * (count - 1)
    while spare > 0:
        movable = [i for i in range(count - 1) if given[i] < bound]
        whole, remaining = sum([loads[i] for i in movable]), spare
        for i in movable:
            addition = min(bound - given[i], max(1, remaining * loads[i] // whole), spare)
            given[i] = given[i] + addition
            spare = spare - addition
    return np.array([bound] + given)


def uneven(key, number_of, total, most, lean):
    if number_of == 2:
        one = jax.random.randint(key, (), max(1, total - most), min(most, total - 1) + 1)
        return jnp.stack([one, total - one])
    tallies = jnp.asarray(profile(number_of, total, most, lean), jnp.int32)
    twos = (number_of - 1) // 2
    source_of, receiver = tallies[1:1 + 2 * twos:2], tallies[2:2 + 2 * twos:2]
    slack = jnp.minimum(source_of - 1, most - receiver)
    passed = jax.random.randint(jax.random.fold_in(key, 1), (twos,), 0, 1 << 20) % (slack + 1)
    tallies = tallies.at[1:1 + 2 * twos:2].set(source_of - passed).at[2:2 + 2 * twos:2].set(receiver + passed)
    return tallies[jax.random.permutation(jax.random.fold_in(key, 2), number_of)]


def scatter_about(stream_key, dims, scale, bound, cuts=(), held_as=jnp.bfloat16):
    array = scale * jax.random.normal(stream_key, dims, jnp.float32)
    if cuts:
        array = array * shard_levels(stream_key, dims, cuts, -0.22, 0.18)
    return jnp.clip(array, -bound, bound).astype(held_as)


def heavy_noise(rng, extent, deviation, bound, cuts, heavy, kind=jnp.bfloat16):
    entries = deviation * jax.random.normal(rng, extent, jnp.float32)
    if cuts:
        entries = entries * shard_levels(rng, extent, cuts, -0.22, 0.18)
    return jnp.clip(with_spikes(entries, jax.random.fold_in(rng, 3), *heavy), -bound, bound).astype(kind)


def setup_inputs(seed: int = 0) -> dict:
    keys = jax.random.split(jax.random.key(seed), 9)
    embeds = scatter_about(keys[0], (2, TOKENS, D), 1.0, 6.0, ((0, 2), (1, 32), (2, 4)))
    lengths = jax.vmap(lambda own: uneven(own, N_DP, ROWS * 5 // 8, SLOT, 2))(jax.random.split(keys[1], N_DP)).reshape((N_DP, N_DP)).astype(jnp.int32)
    owners = jax.vmap(lambda own: jax.random.permutation(own, N_DP))(jax.random.split(keys[2], N_DP)).reshape((N_DP, N_DP)).astype(jnp.int32)
    w_query = scatter_about(keys[3], (2, D, HEADS * HEAD_DIM), D ** -0.5, 0.09375, ((0, 2), (2, 4)))
    w_key = scatter_about(keys[4], (2, D, KV_HEADS * HEAD_DIM), D ** -0.5, 0.09375, ((0, 2), (2, 4)))
    w_value = scatter_about(keys[5], (2, D, KV_HEADS * HEAD_DIM), D ** -0.5, 0.09375, ((0, 2), (2, 4)))
    w_out = scatter_about(keys[6], (2, HEADS * HEAD_DIM, D), (HEADS * HEAD_DIM) ** -0.5, 0.125, ((0, 2), (1, 4)))
    cycle_grad = heavy_noise(keys[7], (2, TOKENS, D), 0.125, 0.75, ((0, 2), (1, 32), (2, 4)), (1, 2, 32, 2.75))
    return dict(embeds=embeds, lengths=lengths, owners=owners, w_query=w_query, w_key=w_key, w_value=w_value, w_out=w_out, cycle_grad=cycle_grad)


eps_norm = 1e-05

def pair_mask(row_count, slot_size):
    query_pos = lax.broadcasted_iota(jnp.int32, (row_count, row_count), 0)
    key_pos = lax.broadcasted_iota(jnp.int32, (row_count, row_count), 1)
    return (query_pos // slot_size == key_pos // slot_size) & (key_pos <= query_pos)

def attend_group(hidden, w_query, w_key, w_value, w_out, allowed):
    row_count = hidden.shape[0]
    kv_count = w_key.shape[1] // HEAD_DIM
    repeat = w_query.shape[1] // w_key.shape[1]
    scale = 1.0 / math.sqrt(HEAD_DIM)
    hidden_wide = hidden.astype(jnp.float32)
    inv_rms = lax.rsqrt(lax.optimization_barrier(jnp.mean(hidden_wide * hidden_wide, axis=1, keepdims=True)) + eps_norm)
    normed_wide = hidden_wide * inv_rms
    normed = normed_wide.astype(jnp.bfloat16)
    query_rows = jnp.dot(normed, w_query, preferred_element_type=jnp.float32).astype(jnp.bfloat16)
    key_rows = jnp.dot(normed, w_key, preferred_element_type=jnp.float32).astype(jnp.bfloat16)
    value_rows = jnp.dot(normed, w_value, preferred_element_type=jnp.float32).astype(jnp.bfloat16)
    query_heads = query_rows.reshape(row_count, kv_count, repeat, HEAD_DIM)
    key_heads = key_rows.reshape(row_count, kv_count, HEAD_DIM)
    value_heads = value_rows.reshape(row_count, kv_count, HEAD_DIM)
    scores = jnp.einsum('qgrd,kgd->grqk', query_heads.astype(jnp.float32), key_heads.astype(jnp.float32)) * scale
    scores = jnp.where(allowed, scores, -jnp.inf)
    raised = jnp.exp(scores)
    attn_probs = raised / lax.optimization_barrier(jnp.sum(raised, axis=3, keepdims=True))
    probs_low = attn_probs.astype(jnp.bfloat16)
    attended = jnp.einsum('grqk,kgd->qgrd', probs_low.astype(jnp.float32), value_heads.astype(jnp.float32))
    attended = attended.reshape(row_count, -1).astype(jnp.bfloat16)
    partial_value = jnp.dot(attended, w_out, preferred_element_type=jnp.float32)
    saved = (normed, normed_wide, inv_rms, query_heads, key_heads, value_heads, attn_probs, probs_low, attended)
    return (partial_value, saved)

def attend_back(grad_full, w_query, w_key, w_value, w_out, saved):
    normed, normed_wide, inv_rms, query_heads, key_heads, value_heads, attn_probs, probs_low, attended = saved
    row_count = grad_full.shape[0]
    scale = 1.0 / math.sqrt(HEAD_DIM)
    contract = (((1,), (1,)), ((), ()))
    d_attended = lax.dot_general(grad_full, w_out, contract, preferred_element_type=jnp.float32).astype(jnp.bfloat16)
    d_heads = d_attended.reshape(query_heads.shape)
    d_value = jnp.einsum('grqk,qgrd->kgd', probs_low.astype(jnp.float32), d_heads.astype(jnp.float32))
    d_value = d_value.reshape(row_count, -1).astype(jnp.bfloat16)
    d_probs = jnp.einsum('qgrd,kgd->grqk', d_heads.astype(jnp.float32), value_heads.astype(jnp.float32))
    d_scores = attn_probs * (d_probs - lax.optimization_barrier(jnp.sum(attn_probs * d_probs, axis=3, keepdims=True))) * scale
    d_scores = d_scores.astype(jnp.bfloat16)
    d_query = jnp.einsum('grqk,kgd->qgrd', d_scores.astype(jnp.float32), key_heads.astype(jnp.float32))
    d_query = d_query.reshape(row_count, -1).astype(jnp.bfloat16)
    d_key = jnp.einsum('grqk,qgrd->kgd', d_scores.astype(jnp.float32), query_heads.astype(jnp.float32))
    d_key = d_key.reshape(row_count, -1).astype(jnp.bfloat16)
    d_normed = lax.dot_general(d_query, w_query, contract, preferred_element_type=jnp.float32)
    d_normed = d_normed + lax.dot_general(d_key, w_key, contract, preferred_element_type=jnp.float32)
    d_normed = d_normed + lax.dot_general(d_value, w_value, contract, preferred_element_type=jnp.float32)
    d_hidden = inv_rms * (d_normed - normed_wide * lax.optimization_barrier(jnp.mean(d_normed * normed_wide, axis=1, keepdims=True)))
    return (d_hidden, jnp.concatenate([d_query, d_key, d_value], axis=1))

def group_weights(weights, group):
    w_query, w_key, w_value, w_out = weights
    query_width = w_query.shape[1] // N_MP
    pair_width = w_key.shape[1] // N_MP
    return (w_query[:, group * query_width:(group + 1) * query_width], w_key[:, group * pair_width:(group + 1) * pair_width], w_value[:, group * pair_width:(group + 1) * pair_width], w_out[group * query_width:(group + 1) * query_width])

def layer_forward(hidden, live_rows, weights, allowed):
    total = jnp.zeros(hidden.shape, jnp.float32)
    for group in range(N_MP):
        partial_value, saved = attend_group(hidden, *group_weights(weights, group), allowed)
        total = total + partial_value
    return (live_rows * (hidden.astype(jnp.float32) + total)).astype(jnp.bfloat16)

def layer_backward(hidden, grad, live_rows, weights, allowed):
    grad_masked = (live_rows * grad.astype(jnp.float32)).astype(jnp.bfloat16)
    total = jnp.zeros(hidden.shape, jnp.float32)
    query_parts, key_parts, value_parts, out_parts = ([], [], [], [])
    contract = (((0,), (0,)), ((), ()))
    for group in range(N_MP):
        pieces = group_weights(weights, group)
        partial_value, saved = attend_group(hidden, *pieces, allowed)
        d_hidden, right_cols = attend_back(grad_masked, *pieces, saved)
        total = total + d_hidden
        query_width = pieces[0].shape[1]
        pair_width = pieces[1].shape[1]
        term_qkv = lax.dot_general(saved[0], right_cols, contract, preferred_element_type=jnp.float32)
        term_out = lax.dot_general(grad_masked, saved[8], contract, preferred_element_type=jnp.float32)
        query_parts.append(term_qkv[:, :query_width])
        key_parts.append(term_qkv[:, query_width:query_width + pair_width])
        value_parts.append(term_qkv[:, query_width + pair_width:])
        out_parts.append(term_out)
    d_input = (grad_masked.astype(jnp.float32) + total).astype(jnp.bfloat16)
    terms = (jnp.concatenate(query_parts, axis=1), jnp.concatenate(key_parts, axis=1), jnp.concatenate(value_parts, axis=1), jnp.concatenate(out_parts, axis=1))
    return (d_input, terms)

def reference(embeds, lengths, owners, w_query, w_key, w_value, w_out, cycle_grad):
    order = jnp.argsort(owners, axis=1).astype(jnp.int32)
    sources = jnp.arange(N_DP, dtype=jnp.int32)
    received = jnp.take_along_axis(lengths, order, axis=1).T
    position = jnp.arange(SLOT, dtype=jnp.int32)
    live = (position[None, None, :] < received[:, :, None]).astype(jnp.float32).reshape(N_DP, ROWS, 1)
    allowed = pair_mask(ROWS, SLOT)
    weights = [(w_query[side], w_key[side], w_value[side], w_out[side]) for side in range(2)]

    def arrange(table):
        slots = table.reshape(N_DP, N_DP, SLOT, D)
        return slots[sources[None, :], order.T].reshape(N_DP, ROWS, D)

    def apply_all(blocks, side_weights):

        def one_block(pair):
            return layer_forward(pair[0], pair[1], side_weights, allowed)
        return lax.map(one_block, (blocks, live))
    moved = [arrange(embeds[side]) for side in range(2)]
    decoded = [apply_all(moved[side], weights[side]) for side in range(2)]
    cycled = [apply_all(decoded[1 - side], weights[side]) for side in range(2)]
    grads_in = [cycle_grad[side].reshape(N_DP, ROWS, D) for side in range(2)]

    def step(carry, blocks):
        live_block = blocks[0]
        decoded_blocks = (blocks[1], blocks[2])
        moved_blocks = (blocks[3], blocks[4])
        grad_blocks = (blocks[5], blocks[6])
        back = []
        second_terms = []
        for side in range(2):
            d_input, terms = layer_backward(decoded_blocks[1 - side], grad_blocks[side], live_block, weights[side], allowed)
            back.append(d_input)
            second_terms.append(terms)
        fronts = []
        new_carry = []
        for side in range(2):
            d_input, terms = layer_backward(moved_blocks[side], back[1 - side], live_block, weights[side], allowed)
            fronts.append(d_input)
            for member in range(4):
                rounded = lax.optimization_barrier((terms[member] + second_terms[side][member]).astype(jnp.bfloat16))
                new_carry.append(carry[side * 4 + member] + rounded.astype(jnp.float32))
        return (tuple(new_carry), (fronts[0], fronts[1]))
    init = []
    for side in range(2):
        init.append(jnp.zeros(w_query.shape[1:], jnp.float32))
        init.append(jnp.zeros(w_key.shape[1:], jnp.float32))
        init.append(jnp.zeros(w_value.shape[1:], jnp.float32))
        init.append(jnp.zeros((D, w_out.shape[1]), jnp.float32))
    carry, fronts = lax.scan(step, tuple(init), (live, decoded[0], decoded[1], moved[0], moved[1], grads_in[0], grads_in[1]))

    def restore(front):
        blocks = front.reshape(N_DP, N_DP, SLOT, D)
        return blocks[owners, sources[:, None]].reshape(TOKENS, D)
    cycled_out = jnp.stack([cycled[side].reshape(TOKENS, D) for side in range(2)])
    embed_grad = jnp.stack([restore(fronts[side]) for side in range(2)])
    grad_query = jnp.stack([carry[0], carry[4]])
    grad_key = jnp.stack([carry[1], carry[5]])
    grad_value = jnp.stack([carry[2], carry[6]])
    grad_output = jnp.stack([carry[3], carry[7]])
    return (cycled_out, embed_grad, grad_query, grad_key, grad_value, grad_output)
```

```python
import math

import jax
import jax.numpy as jnp
from jax import lax
from jax.experimental import pallas as pl
from jax.experimental.pallas import tpu as pltpu
from jax.sharding import PartitionSpec as P

HEAD_DIM = 128
SLOT = 6
LIVE = 120
EPS = 1e-05
SCALE = 1.0 / math.sqrt(HEAD_DIM)
F32 = jnp.float32
BF16 = jnp.bfloat16
NT = (((1,), (1,)), ((), ()))
TN = (((0,), (0,)), ((), ()))


def dot(a, b):
    return jnp.dot(a, b, preferred_element_type=F32)


def dot_nt(a, b):
    return lax.dot_general(a, b, NT, preferred_element_type=F32)


def dot_tn(a, b):
    return lax.dot_general(a, b, TN, preferred_element_type=F32)


def shift(block, axis, by):
    count = lax.axis_size(axis)
    return lax.ppermute(block, axis, [(i, (i + by) % count) for i in range(count)])


def widen(shard):
    me = lax.axis_index("mp")
    width = shard.shape[1]
    across = shift(shard, "mp", 2)
    right = shift(shard, "mp", 1)
    left = shift(shard, "mp", 3)
    full = jnp.zeros((shard.shape[0], 4 * width), shard.dtype)
    for block, by in ((shard, 0), (right, 3), (left, 1), (across, 2)):
        full = lax.dynamic_update_slice(full, block, (0, (me + by) % 4 * width))
    return full


def narrow(partial):
    me = lax.axis_index("mp")
    width = partial.shape[1] // 4

    def block(by):
        return lax.dynamic_slice(
            partial, (0, (me + by) % 4 * width), (partial.shape[0], width)
        )

    across = shift(block(2).astype(BF16), "mp", 2)
    right = shift(block(1).astype(BF16), "mp", 1)
    left = shift(block(3).astype(BF16), "mp", 3)
    return block(0) + right.astype(F32) + left.astype(F32) + across.astype(F32)


def partner(block):
    return lax.ppermute(block, "section", [(0, 1), (1, 0)])


def other_core(block):
    count = lax.axis_size("dp")
    return lax.ppermute(block, "dp", [(i, i ^ 1) for i in range(count)])


def pick_kernel(which, a_ref, out_ref):
    groups = out_ref.shape[1] // 128
    first = which[0] == 0
    for j in range(groups):
        even = a_ref[:, 2 * j * 128 : (2 * j + 1) * 128]
        odd = a_ref[:, (2 * j + 1) * 128 : (2 * j + 2) * 128]
        out_ref[:, j * 128 : (j + 1) * 128] = jnp.where(first, even, odd)


def pick(a, which):
    rows, cols = a.shape
    return pl.pallas_call(
        pick_kernel,
        out_shape=jax.ShapeDtypeStruct((rows, cols // 2), a.dtype),
        in_specs=[
            pl.BlockSpec(memory_space=pltpu.SMEM),
            pl.BlockSpec(memory_space=pltpu.VMEM),
        ],
        out_specs=pl.BlockSpec(memory_space=pltpu.VMEM),
        cost_estimate=pl.CostEstimate(
            flops=rows * cols, bytes_accessed=3 * rows * cols, transcendentals=0
        ),
        name="pick",
    )(which.reshape(1), a)


def grads_kernel(norm_ref, right_ref, grad_ref, att_ref, out_ref):
    cols = right_ref.shape[1]
    out_ref[:, :cols] = dot_tn(norm_ref[...], right_ref[...]).astype(BF16)
    out_ref[:, cols:] = dot_tn(grad_ref[...], att_ref[...]).astype(BF16)


def weight_grads(norm, right, grad, att):
    rows, height = norm.shape
    cols = right.shape[1] + att.shape[1]
    step = 256
    return pl.pallas_call(
        grads_kernel,
        grid=(height // step,),
        out_shape=jax.ShapeDtypeStruct((height, cols), BF16),
        in_specs=[
            pl.BlockSpec((rows, step), lambda i: (0, i)),
            pl.BlockSpec(right.shape, lambda i: (0, 0)),
            pl.BlockSpec((rows, step), lambda i: (0, i)),
            pl.BlockSpec(att.shape, lambda i: (0, 0)),
        ],
        out_specs=pl.BlockSpec((step, cols), lambda i: (i, 0)),
        cost_estimate=pl.CostEstimate(
            flops=2 * rows * height * cols,
            bytes_accessed=2 * (rows * (2 * height + cols) + height * cols),
            transcendentals=0,
        ),
        name="weight_grads",
    )(norm, right, grad, att)


def attend(full, w_query, w_key, w_value, allowed):
    wide = full.astype(F32)
    inv_rms = lax.rsqrt(jnp.mean(wide * wide, axis=1, keepdims=True) + EPS)
    normed = (wide * inv_rms).astype(BF16)
    query = dot(normed, w_query).astype(BF16)
    key = dot(normed, w_key).astype(BF16)
    value = dot(normed, w_value).astype(BF16)
    heads = query.reshape(query.shape[0], -1, HEAD_DIM)
    scores = jnp.einsum("qrd,kd->rqk", heads, key, preferred_element_type=F32) * SCALE
    raised = jnp.exp(jnp.where(allowed, scores, -jnp.inf))
    probs = raised / jnp.sum(raised, axis=2, keepdims=True)
    probs_low = probs.astype(BF16)
    attended = jnp.einsum("rqk,kd->qrd", probs_low, value, preferred_element_type=F32)
    attended = attended.reshape(query.shape).astype(BF16)
    return dict(
        full=full,
        inv_rms=inv_rms,
        normed=normed,
        heads=heads,
        key=key,
        value=value,
        probs=probs,
        probs_low=probs_low,
        attended=attended,
    )


def attend_back(grad_full, w_query, w_key, w_value, w_out, saved):
    rows = grad_full.shape[0]
    probs, key, value, heads = saved["probs"], saved["key"], saved["value"], saved["heads"]
    d_heads = dot_nt(grad_full, w_out).astype(BF16).reshape(heads.shape)
    d_value = jnp.einsum("rqk,qrd->kd", saved["probs_low"], d_heads, preferred_element_type=F32)
    d_value = d_value.astype(BF16)
    d_probs = jnp.einsum("qrd,kd->rqk", d_heads, value, preferred_element_type=F32)
    d_scores = probs * (d_probs - jnp.sum(probs * d_probs, axis=2, keepdims=True)) * SCALE
    d_scores = d_scores.astype(BF16)
    d_query = jnp.einsum("rqk,kd->qrd", d_scores, key, preferred_element_type=F32)
    d_query = d_query.reshape(rows, -1).astype(BF16)
    d_key = jnp.einsum("rqk,qrd->kd", d_scores, heads, preferred_element_type=F32).astype(BF16)
    d_normed = dot_nt(d_query, w_query) + dot_nt(d_key, w_key) + dot_nt(d_value, w_value)
    wide = saved["full"].astype(F32) * saved["inv_rms"]
    d_full = saved["inv_rms"] * (
        d_normed - wide * jnp.mean(d_normed * wide, axis=1, keepdims=True)
    )
    return d_full, jnp.concatenate([d_query, d_key, d_value], axis=1)


def on_device(embeds, lengths, owners, w_query, w_key, w_value, w_out, cycle_grad):
    pairs = lax.axis_size("dp")
    dp_self = lax.axis_index("dp")
    core = dp_self % 2
    rows, width = embeds.shape[1:]
    w_query, w_key, w_value, w_out = w_query[0], w_key[0], w_value[0], w_out[0]

    own_len = lax.dynamic_slice_in_dim(lengths, dp_self, 1, 0)[0]
    own_owner = lax.dynamic_slice_in_dim(owners, dp_self, 1, 0)[0]
    slots = jnp.arange(pairs, dtype=jnp.int32)
    ends = jnp.sum(jnp.where(slots[None, :] <= slots[:, None], own_len[None, :], 0), axis=1)
    starts = ends - own_len
    live_ids = jnp.arange(LIVE, dtype=jnp.int32)
    in_slot = (live_ids[:, None] >= starts[None, :]) & (live_ids[:, None] < ends[None, :])

    def of_slot(table):
        return jnp.sum(jnp.where(in_slot, table[None, :], 0), axis=1)

    slot = of_slot(slots)
    place = live_ids - of_slot(starts)
    at_source = slot * SLOT + place
    at_owner = of_slot(own_owner) * SLOT + place
    row_ids = jnp.arange(rows, dtype=jnp.int32)
    from_source = (at_source[:, None] == row_ids[None, :]).astype(BF16)
    from_owner = (at_owner[:, None] == row_ids[None, :]).astype(BF16)
    allowed = (slot[:, None] == slot[None, :]) & (live_ids[None, :] <= live_ids[:, None])

    def regroup(block):
        split = block.reshape(pairs, SLOT, width)
        return lax.all_to_all(split, "dp", split_axis=0, concat_axis=0, tiled=True).reshape(
            rows, width
        )

    grad_rows = regroup(cycle_grad[0])
    moved = dot(from_source, embeds[0]).astype(BF16)
    moved_full = widen(moved)
    first = attend(moved_full, w_query, w_key, w_value, allowed)
    branch = narrow(dot(first["attended"], w_out))
    decoded = (moved.astype(F32) + branch).astype(BF16)
    grad = dot(from_owner, grad_rows).astype(BF16)
    decoded, grad = lax.optimization_barrier((decoded, grad))
    incoming = partner(decoded)
    grad_full = widen(grad)
    incoming, grad_full = lax.optimization_barrier((incoming, grad_full))
    incoming_full = widen(incoming)
    second = attend(incoming_full, w_query, w_key, w_value, allowed)
    d_second, cols_second = attend_back(grad_full, w_query, w_key, w_value, w_out, second)
    back = (grad.astype(F32) + narrow(d_second)).astype(BF16)
    back, late = lax.optimization_barrier((back, second["attended"]))
    ret = partner(back)
    cycled = (incoming.astype(F32) + narrow(dot(late, w_out))).astype(BF16)
    ret, cycled = lax.optimization_barrier((ret, cycled))
    ret_full = widen(ret)
    cycled_rows = regroup(dot_tn(from_owner, cycled).astype(BF16))
    d_first, cols_first = attend_back(ret_full, w_query, w_key, w_value, w_out, first)
    front = (ret.astype(F32) + narrow(d_first)).astype(BF16)
    restored = dot_tn(from_source, front).astype(BF16)

    def both(left):
        mine = pick(left, core)
        return [mine, other_core(pick(left, 1 - core))]

    norm = jnp.concatenate(both(first["normed"]) + both(second["normed"]), axis=0)
    left = jnp.concatenate(both(ret_full) + both(grad_full), axis=0)
    right = jnp.concatenate(
        [cols_first, other_core(cols_first), cols_second, other_core(cols_second)], axis=0
    )
    att = jnp.concatenate(
        [first["attended"], other_core(first["attended"]), late, other_core(late)], axis=0
    )
    same_core = [[2 * i + c for i in range(pairs // 2)] for c in range(2)]
    summed = lax.psum_scatter(
        weight_grads(norm, right, left, att),
        "dp",
        scatter_dimension=0,
        tiled=True,
        axis_index_groups=same_core,
    ).astype(F32)
    wq, wk = w_query.shape[1], w_key.shape[1]
    return (
        cycled_rows[None],
        restored[None],
        summed[None, :, :wq],
        summed[None, :, wq : wq + wk],
        summed[None, :, wq + wk : wq + 2 * wk],
        summed[None, :, wq + 2 * wk :],
    )


def solution(mesh):
    rows = P("section", "dp", "mp")
    columns = P("section", None, "mp")
    return jax.shard_map(
        on_device,
        mesh=mesh,
        in_specs=(rows, P(), P(), columns, columns, columns, P("section", "mp", None), rows),
        out_specs=(rows,) * 6,
        check_vma=False,
    )
```

```python
import functools
import math

import jax
import jax.numpy as jnp
from jax import lax
from jax.experimental import pallas as pl
from jax.experimental.pallas import tpu as pltpu
from jax.sharding import PartitionSpec as P

HEAD_DIM = 128
SLOT = 6
LIVE = 120
EPS = 1e-05
SCALE = 1.0 / math.sqrt(HEAD_DIM)
F32 = jnp.float32
BF16 = jnp.bfloat16
NT = (((1,), (1,)), ((), ()))
TN = (((0,), (0,)), ((), ()))


def dot(a, b):
    return jnp.dot(a, b, preferred_element_type=F32)


def dot_nt(a, b):
    return lax.dot_general(a, b, NT, preferred_element_type=F32)


def dot_tn(a, b):
    return lax.dot_general(a, b, TN, preferred_element_type=F32)


def shift(block, axis, by):
    count = lax.axis_size(axis)
    return lax.ppermute(block, axis, [(i, (i + by) % count) for i in range(count)])


def widen(shard):
    me = lax.axis_index("mp")
    width = shard.shape[1]
    across = shift(shard, "mp", 2)
    right = shift(shard, "mp", 1)
    left = shift(shard, "mp", 3)
    full = jnp.zeros((shard.shape[0], 4 * width), shard.dtype)
    for block, by in ((shard, 0), (right, 3), (left, 1), (across, 2)):
        full = lax.dynamic_update_slice(full, block, (0, (me + by) % 4 * width))
    return full


def narrow(partial):
    me = lax.axis_index("mp")
    width = partial.shape[1] // 4

    def block(by):
        return lax.dynamic_slice(
            partial, (0, (me + by) % 4 * width), (partial.shape[0], width)
        )

    across = shift(block(2).astype(BF16), "mp", 2)
    right = shift(block(1).astype(BF16), "mp", 1)
    left = shift(block(3).astype(BF16), "mp", 3)
    return block(0) + right.astype(F32) + left.astype(F32) + across.astype(F32)


def partner(block):
    return lax.ppermute(block, "section", [(0, 1), (1, 0)])


def grads_kernel(base, right_at, *refs):
    out_ref = refs[-1]
    total = refs[-2][...] if base else None
    for k in range(refs[0].shape[0]):
        term = dot_tn(refs[0][k], refs[1][k, :, right_at : right_at + out_ref.shape[1]])
        total = term if total is None else total + term
    out_ref[...] = total.astype(out_ref.dtype)


def weight_grads(left, right, right_at, cols, base, dtype):
    count, rows, _ = left.shape
    height, step = 1024, 256
    specs = [
        pl.BlockSpec((count, rows, step), lambda i: (0, 0, i)),
        pl.BlockSpec(right.shape, lambda i: (0, 0, 0)),
    ]
    tile = pl.BlockSpec((step, cols), lambda i: (i, 0))
    extra = [] if base is None else [base]
    return pl.pallas_call(
        functools.partial(grads_kernel, base is not None, right_at),
        grid=(height // step,),
        out_shape=jax.ShapeDtypeStruct((height, cols), dtype),
        in_specs=specs + [tile] * len(extra),
        out_specs=tile,
        cost_estimate=pl.CostEstimate(
            flops=2 * count * rows * height * cols,
            bytes_accessed=2 * count * rows * (height + cols) + 4 * height * cols,
            transcendentals=0,
        ),
        name="weight_grads",
    )(left, right, *extra)


def groups_along(stride, size):
    count = lax.axis_size("dp")
    heads = [i for i in range(count) if i // stride % size == 0]
    return [[head + k * stride for k in range(size)] for head in heads]


def swap_along(block, stride, size):
    return lax.all_to_all(
        block,
        "dp",
        split_axis=0,
        concat_axis=0,
        tiled=True,
        axis_index_groups=groups_along(stride, size),
    )


def shift_part(block, stride, size, by):
    count = lax.axis_size("dp")
    route = []
    for i in range(count):
        part = i // stride % size
        route.append((i, i + ((part + by) % size - part) * stride))
    return lax.ppermute(block, "dp", route)


def part_of(parts, at):
    return lax.dynamic_index_in_dim(parts, at % 4, 0, keepdims=False)


def features_along_z(left):
    return swap_along(left.reshape(left.shape[0], 4, -1).transpose(1, 0, 2), 8, 4)


def copies_along_z(right):
    return swap_along(jnp.broadcast_to(right[None], (4,) + right.shape), 8, 4)


def features_along_z_shared(left):
    z, me = lax.axis_index("dp") // 8, lax.axis_index("mp")
    rows, width = left.shape[0], left.shape[1] // 16
    parts = jnp.stack(
        [lax.dynamic_slice(left, (0, (4 * k + me) * width), (rows, width)) for k in range(4)]
    )
    held = parts
    for by in (2, 1, 3):
        came = shift_part(part_of(parts, z + by), 8, 4, by)
        held = lax.dynamic_update_slice(held, came[None], ((z - by) % 4, 0, 0))
    return widen(held.reshape(4 * rows, width)).reshape(4, rows, 4 * width)


def sum_over_y_and_core(partial):
    height = partial.shape[0] // 4
    me = lax.axis_index("dp")
    y, core = me // 2 % 4, me % 2
    parts = partial.reshape(4, height, -1)
    total = part_of(parts, y).astype(F32)
    for by in (2, 1, 3):
        total = total + shift_part(part_of(parts, y + by), 2, 4, by).astype(F32)
    half = height // 2
    sent = lax.dynamic_slice_in_dim(total, (1 - core) * half, half, 0).astype(BF16)
    kept = lax.dynamic_slice_in_dim(total, core * half, half, 0)
    return kept + shift_part(sent, 1, 2, 1).astype(F32)


def attend(full, w_query, w_key, w_value, allowed):
    wide = full.astype(F32)
    inv_rms = lax.rsqrt(jnp.mean(wide * wide, axis=1, keepdims=True) + EPS)
    normed = (wide * inv_rms).astype(BF16)
    query = dot(normed, w_query).astype(BF16)
    key = dot(normed, w_key).astype(BF16)
    value = dot(normed, w_value).astype(BF16)
    heads = query.reshape(query.shape[0], -1, HEAD_DIM)
    scores = jnp.einsum("qrd,kd->rqk", heads, key, preferred_element_type=F32) * SCALE
    raised = jnp.exp(jnp.where(allowed, scores, -jnp.inf))
    probs = raised / jnp.sum(raised, axis=2, keepdims=True)
    probs_low = probs.astype(BF16)
    attended = jnp.einsum("rqk,kd->qrd", probs_low, value, preferred_element_type=F32)
    attended = attended.reshape(query.shape).astype(BF16)
    return dict(
        full=full,
        inv_rms=inv_rms,
        normed=normed,
        heads=heads,
        key=key,
        value=value,
        probs=probs,
        probs_low=probs_low,
        attended=attended,
    )


def attend_back(grad_full, w_query, w_key, w_value, w_out, saved):
    rows = grad_full.shape[0]
    probs, key, value, heads = saved["probs"], saved["key"], saved["value"], saved["heads"]
    d_heads = dot_nt(grad_full, w_out).astype(BF16).reshape(heads.shape)
    d_value = jnp.einsum("rqk,qrd->kd", saved["probs_low"], d_heads, preferred_element_type=F32)
    d_value = d_value.astype(BF16)
    d_probs = jnp.einsum("qrd,kd->rqk", d_heads, value, preferred_element_type=F32)
    d_scores = probs * (d_probs - jnp.sum(probs * d_probs, axis=2, keepdims=True)) * SCALE
    d_scores = d_scores.astype(BF16)
    d_query = jnp.einsum("rqk,kd->qrd", d_scores, key, preferred_element_type=F32)
    d_query = d_query.reshape(rows, -1).astype(BF16)
    d_key = jnp.einsum("rqk,qrd->kd", d_scores, heads, preferred_element_type=F32).astype(BF16)
    d_normed = dot_nt(d_query, w_query) + dot_nt(d_key, w_key) + dot_nt(d_value, w_value)
    wide = saved["full"].astype(F32) * saved["inv_rms"]
    d_full = saved["inv_rms"] * (
        d_normed - wide * jnp.mean(d_normed * wide, axis=1, keepdims=True)
    )
    return d_full, jnp.concatenate([d_query, d_key, d_value], axis=1)


def on_device(embeds, lengths, owners, w_query, w_key, w_value, w_out, cycle_grad):
    pairs = lax.axis_size("dp")
    dp_self = lax.axis_index("dp")
    rows, width = embeds.shape[1:]
    w_query, w_key, w_value, w_out = w_query[0], w_key[0], w_value[0], w_out[0]

    own_len = lax.dynamic_slice_in_dim(lengths, dp_self, 1, 0)[0]
    own_owner = lax.dynamic_slice_in_dim(owners, dp_self, 1, 0)[0]
    slots = jnp.arange(pairs, dtype=jnp.int32)
    ends = jnp.sum(jnp.where(slots[None, :] <= slots[:, None], own_len[None, :], 0), axis=1)
    starts = ends - own_len
    live_ids = jnp.arange(LIVE, dtype=jnp.int32)
    in_slot = (live_ids[:, None] >= starts[None, :]) & (live_ids[:, None] < ends[None, :])

    def of_slot(table):
        return jnp.sum(jnp.where(in_slot, table[None, :], 0), axis=1)

    slot = of_slot(slots)
    place = live_ids - of_slot(starts)
    at_source = slot * SLOT + place
    at_owner = of_slot(own_owner) * SLOT + place
    row_ids = jnp.arange(rows, dtype=jnp.int32)
    from_source = (at_source[:, None] == row_ids[None, :]).astype(BF16)
    from_owner = (at_owner[:, None] == row_ids[None, :]).astype(BF16)
    allowed = (slot[:, None] == slot[None, :]) & (live_ids[None, :] <= live_ids[:, None])

    def regroup(block):
        split = block.reshape(pairs, SLOT, width)
        return lax.all_to_all(split, "dp", split_axis=0, concat_axis=0, tiled=True).reshape(
            rows, width
        )

    barrier = lax.optimization_barrier
    wq, wk = w_query.shape[1], w_key.shape[1]
    grad_rows = regroup(cycle_grad[0])
    moved = dot(from_source, embeds[0]).astype(BF16)
    moved_full = widen(moved)
    first = attend(moved_full, w_query, w_key, w_value, allowed)
    norm_first = features_along_z(first["normed"])
    branch = narrow(dot(first["attended"], w_out))
    att_first = copies_along_z(first["attended"])
    decoded = (moved.astype(F32) + branch).astype(BF16)
    grad = dot(from_owner, grad_rows).astype(BF16)
    decoded, grad, norm_first = barrier((decoded, grad, norm_first))
    incoming = partner(decoded)
    grad_full = widen(grad)
    incoming, grad_full = barrier((incoming, grad_full))
    grad_second = features_along_z(grad_full)
    incoming_full = widen(incoming)
    second = attend(incoming_full, w_query, w_key, w_value, allowed)
    norm_second = features_along_z(second["normed"])
    d_second, cols_second = attend_back(grad_full, w_query, w_key, w_value, w_out, second)
    back = (grad.astype(F32) + narrow(d_second)).astype(BF16)
    back, late, cols_second, norm_second, grad_second, att_first = barrier(
        (back, second["attended"], cols_second, norm_second, grad_second, att_first)
    )
    ret = partner(back)
    cycled = (incoming.astype(F32) + narrow(dot(late, w_out))).astype(BF16)
    right_second = jnp.concatenate([late, cols_second], axis=1)
    ret, cycled, right_second = barrier((ret, cycled, right_second))
    ret_full = widen(ret)
    right_second = copies_along_z(right_second)
    grad_first = features_along_z_shared(ret_full)
    d_first, cols_first = attend_back(ret_full, w_query, w_key, w_value, w_out, first)
    right_second, cols_first = barrier((right_second, cols_first))
    cols_first = copies_along_z(cols_first)
    out_second = weight_grads(grad_second, right_second, 0, wq, None, F32)
    qkv_second = weight_grads(norm_second, right_second, wq, wq + 2 * wk, None, F32)
    front = (ret.astype(F32) + narrow(d_first)).astype(BF16)
    restored = dot_tn(from_source, front).astype(BF16)
    out_sum = sum_over_y_and_core(weight_grads(grad_first, att_first, 0, wq, out_second, BF16))
    cols_first, cycled = barrier((cols_first, cycled))
    cycled_rows = regroup(dot_tn(from_owner, cycled).astype(BF16))
    qkv_sum = sum_over_y_and_core(
        weight_grads(norm_first, cols_first, 0, wq + 2 * wk, qkv_second, BF16)
    )
    return (
        cycled_rows[None],
        restored[None],
        qkv_sum[None, :, :wq],
        qkv_sum[None, :, wq : wq + wk],
        qkv_sum[None, :, wq + wk :],
        out_sum[None],
    )


def solution(mesh):
    rows = P("section", "dp", "mp")
    columns = P("section", None, "mp")
    return jax.shard_map(
        on_device,
        mesh=mesh,
        in_specs=(rows, P(), P(), columns, columns, columns, P("section", "mp", None), rows),
        out_specs=(rows,) * 6,
        check_vma=False,
    )
```

```python
import math

import jax
import jax.numpy as jnp
from jax import lax
from jax.experimental import pallas as pl
from jax.experimental.pallas import tpu as pltpu
from jax.sharding import PartitionSpec as P

HEAD_DIM = 128
SLOT = 6
LIVE = 120
EPS = 1e-05
SCALE = 1.0 / math.sqrt(HEAD_DIM)
F32 = jnp.float32
BF16 = jnp.bfloat16
NT = (((1,), (1,)), ((), ()))
TN = (((0,), (0,)), ((), ()))


def dot(a, b):
    return jnp.dot(a, b, preferred_element_type=F32)


def dot_nt(a, b):
    return lax.dot_general(a, b, NT, preferred_element_type=F32)


def dot_tn(a, b):
    return lax.dot_general(a, b, TN, preferred_element_type=F32)


def shift(block, axis, by):
    count = lax.axis_size(axis)
    return lax.ppermute(block, axis, [(i, (i + by) % count) for i in range(count)])


def widen(shard):
    me = lax.axis_index("mp")
    width = shard.shape[1]
    across = shift(shard, "mp", 2)
    right = shift(shard, "mp", 1)
    left = shift(shard, "mp", 3)
    full = jnp.zeros((shard.shape[0], 4 * width), shard.dtype)
    for block, by in ((shard, 0), (right, 3), (left, 1), (across, 2)):
        full = lax.dynamic_update_slice(full, block, (0, (me + by) % 4 * width))
    return full


def narrow(partial):
    me = lax.axis_index("mp")
    width = partial.shape[1] // 4

    def block(by):
        return lax.dynamic_slice(
            partial, (0, (me + by) % 4 * width), (partial.shape[0], width)
        )

    across = shift(block(2).astype(BF16), "mp", 2)
    right = shift(block(1).astype(BF16), "mp", 1)
    left = shift(block(3).astype(BF16), "mp", 3)
    return block(0) + right.astype(F32) + left.astype(F32) + across.astype(F32)


def partner(block):
    return lax.ppermute(block, "section", [(0, 1), (1, 0)])


def shift_part(block, stride, size, by):
    count = lax.axis_size("dp")
    route = []
    for i in range(count):
        part = i // stride % size
        route.append((i, i + ((part + by) % size - part) * stride))
    return lax.ppermute(block, "dp", route)


def other_core(block):
    return shift_part(block, 1, 2, 1)


def pick_kernel(which, a_ref, out_ref):
    for j in range(16):
        at = pl.multiple_of((j % 4 * 8 + j // 4 * 2 + which[0]) * 128, 128)
        out_ref[:, j * 128 : (j + 1) * 128] = a_ref[:, pl.ds(at, 128)]


def pick(a, which):
    rows, cols = a.shape
    return pl.pallas_call(
        pick_kernel,
        out_shape=jax.ShapeDtypeStruct((rows, cols // 2), a.dtype),
        in_specs=[
            pl.BlockSpec(memory_space=pltpu.SMEM),
            pl.BlockSpec(memory_space=pltpu.VMEM),
        ],
        out_specs=pl.BlockSpec(memory_space=pltpu.VMEM),
        cost_estimate=pl.CostEstimate(
            flops=rows * cols, bytes_accessed=3 * rows * cols, transcendentals=0
        ),
        name="pick",
    )(which.reshape(1), a)


def stack(blocks):
    rows, cols = blocks[0].shape
    held = jnp.zeros((len(blocks) * rows, cols), blocks[0].dtype)
    for k, block in enumerate(blocks):
        held = lax.dynamic_update_slice(held, block, (k * rows, 0))
    return held


def sum_along(total, at, stride):
    parts = total.reshape(4, total.shape[0] // 4, -1)

    def part(by):
        return lax.dynamic_index_in_dim(parts, (at + by) % 4, 0, keepdims=False)

    held = part(0).astype(F32)
    for by in (2, 1, 3):
        held = held + shift_part(part(by).astype(BF16), stride, 4, by).astype(F32)
    return held


def sum_over_y(total):
    return sum_along(total, lax.axis_index("dp") // 2, 2)


def sum_over_z(total):
    return sum_along(total, lax.axis_index("dp") // 8, 8)


def attend(full, w_query, w_key, w_value, allowed):
    wide = full.astype(F32)
    inv_rms = lax.rsqrt(jnp.mean(wide * wide, axis=1, keepdims=True) + EPS)
    normed = (wide * inv_rms).astype(BF16)
    query = dot(normed, w_query).astype(BF16)
    key = dot(normed, w_key).astype(BF16)
    value = dot(normed, w_value).astype(BF16)
    heads = query.reshape(query.shape[0], -1, HEAD_DIM)
    scores = jnp.einsum("qrd,kd->rqk", heads, key, preferred_element_type=F32) * SCALE
    raised = jnp.exp(jnp.where(allowed, scores, -jnp.inf))
    probs = raised / jnp.sum(raised, axis=2, keepdims=True)
    probs_low = probs.astype(BF16)
    attended = jnp.einsum("rqk,kd->qrd", probs_low, value, preferred_element_type=F32)
    attended = attended.reshape(query.shape).astype(BF16)
    return dict(
        full=full,
        inv_rms=inv_rms,
        normed=normed,
        heads=heads,
        key=key,
        value=value,
        probs=probs,
        probs_low=probs_low,
        attended=attended,
    )


def attend_back(grad_full, w_out, saved):
    rows = grad_full.shape[0]
    probs, key, value, heads = saved["probs"], saved["key"], saved["value"], saved["heads"]
    d_heads = dot_nt(grad_full, w_out).astype(BF16).reshape(heads.shape)
    d_value = jnp.einsum("rqk,qrd->kd", saved["probs_low"], d_heads, preferred_element_type=F32)
    d_value = d_value.astype(BF16)
    d_probs = jnp.einsum("qrd,kd->rqk", d_heads, value, preferred_element_type=F32)
    d_scores = probs * (d_probs - jnp.sum(probs * d_probs, axis=2, keepdims=True)) * SCALE
    d_scores = d_scores.astype(BF16)
    d_query = jnp.einsum("rqk,kd->qrd", d_scores, key, preferred_element_type=F32)
    d_query = d_query.reshape(rows, -1).astype(BF16)
    d_key = jnp.einsum("rqk,qrd->kd", d_scores, heads, preferred_element_type=F32).astype(BF16)
    return d_query, d_key, d_value


def norm_back(d_cols, w_query, w_key, w_value, saved):
    d_query, d_key, d_value = d_cols
    d_normed = dot_nt(d_query, w_query) + dot_nt(d_key, w_key) + dot_nt(d_value, w_value)
    wide = saved["full"].astype(F32) * saved["inv_rms"]
    return saved["inv_rms"] * (
        d_normed - wide * jnp.mean(d_normed * wide, axis=1, keepdims=True)
    )


def on_device(embeds, lengths, owners, w_query, w_key, w_value, w_out, cycle_grad):
    pairs = lax.axis_size("dp")
    dp_self = lax.axis_index("dp")
    core = dp_self % 2
    rows, width = embeds.shape[1:]
    w_query, w_key, w_value, w_out = w_query[0], w_key[0], w_value[0], w_out[0]

    own_len = lax.dynamic_slice_in_dim(lengths, dp_self, 1, 0)[0]
    own_owner = lax.dynamic_slice_in_dim(owners, dp_self, 1, 0)[0]
    slots = jnp.arange(pairs, dtype=jnp.int32)
    ends = jnp.sum(jnp.where(slots[None, :] <= slots[:, None], own_len[None, :], 0), axis=1)
    starts = ends - own_len
    live_ids = jnp.arange(LIVE, dtype=jnp.int32)
    in_slot = (live_ids[:, None] >= starts[None, :]) & (live_ids[:, None] < ends[None, :])

    def of_slot(table):
        return jnp.sum(jnp.where(in_slot, table[None, :], 0), axis=1)

    slot = of_slot(slots)
    place = live_ids - of_slot(starts)
    at_source = slot * SLOT + place
    at_owner = of_slot(own_owner) * SLOT + place
    row_ids = jnp.arange(rows, dtype=jnp.int32)
    from_source = (at_source[:, None] == row_ids[None, :]).astype(BF16)
    from_owner = (at_owner[:, None] == row_ids[None, :]).astype(BF16)
    allowed = (slot[:, None] == slot[None, :]) & (live_ids[None, :] <= live_ids[:, None])

    def regroup(block):
        split = block.reshape(pairs, SLOT, width)
        return lax.all_to_all(split, "dp", split_axis=0, concat_axis=0, tiled=True).reshape(
            rows, width
        )

    barrier = lax.optimization_barrier
    wq, wk = w_query.shape[1], w_key.shape[1]

    def left_pair(left):
        return [pick(left, core), other_core(pick(left, 1 - core))]

    def right_pair(right):
        return [right, other_core(right)]

    grad_rows = regroup(cycle_grad[0])
    moved = dot(from_source, embeds[0]).astype(BF16)
    moved_full = widen(moved)
    first = attend(moved_full, w_query, w_key, w_value, allowed)
    branch = narrow(dot(first["attended"], w_out))
    decoded = (moved.astype(F32) + branch).astype(BF16)
    grad = dot(from_owner, grad_rows).astype(BF16)
    decoded, grad, norm_first, att_first = barrier(
        (decoded, grad, first["normed"], first["attended"])
    )
    incoming = partner(decoded)
    grad_full = widen(grad)
    norm_first = left_pair(norm_first)
    att_first = right_pair(att_first)
    incoming, grad_full, norm_first, att_first = barrier(
        (incoming, grad_full, norm_first, att_first)
    )
    incoming_full = widen(incoming)
    second = attend(incoming_full, w_query, w_key, w_value, allowed)
    cols_second = attend_back(grad_full, w_out, second)
    d_second = norm_back(cols_second, w_query, w_key, w_value, second)
    back = (grad.astype(F32) + narrow(d_second)).astype(BF16)
    back, late, norm_second, cols_second = barrier(
        (back, second["attended"], second["normed"], cols_second)
    )
    ret = partner(back)
    cycled = (incoming.astype(F32) + narrow(dot(late, w_out))).astype(BF16)
    ret, cycled, late, norm_second, cols_second, grad_left = barrier(
        (ret, cycled, late, norm_second, cols_second, grad_full)
    )
    ret_full = widen(ret)
    cycled_rows = regroup(dot_tn(from_owner, cycled).astype(BF16))
    att = att_first + right_pair(late)
    norm = stack(norm_first + left_pair(norm_second))
    cols_second = right_pair(jnp.concatenate(cols_second, axis=1))
    grad_left = left_pair(grad_left)
    cols_first = attend_back(ret_full, w_out, first)
    out_part = dot_tn(stack(left_pair(ret_full) + grad_left), stack(att)).astype(BF16)
    out_part, cols_first, cycled_rows = barrier((out_part, cols_first, cycled_rows))
    rights = stack(right_pair(jnp.concatenate(cols_first, axis=1)) + cols_second)
    qkv_part = dot_tn(norm, rights).astype(BF16)
    qkv_part, cols_first = barrier((qkv_part, cols_first))
    d_first = norm_back(cols_first, w_query, w_key, w_value, first)
    out_sum = sum_over_y(out_part)
    d_first, out_sum = barrier((d_first, out_sum))
    out_sum = sum_over_z(out_sum)
    qkv_sum = sum_over_z(sum_over_y(qkv_part))
    front = (ret.astype(F32) + narrow(d_first)).astype(BF16)
    restored = dot_tn(from_source, front).astype(BF16)
    return (
        cycled_rows[None],
        restored[None],
        qkv_sum[None, :, :wq],
        qkv_sum[None, :, wq : wq + wk],
        qkv_sum[None, :, wq + wk :],
        out_sum[None],
    )


def solution(mesh):
    rows = P("section", "dp", "mp")
    columns = P("section", None, "mp")
    return jax.shard_map(
        on_device,
        mesh=mesh,
        in_specs=(rows, P(), P(), columns, columns, columns, P("section", "mp", None), rows),
        out_specs=(rows,) * 6,
        check_vma=False,
    )
```

```python
import math

import jax
import jax.numpy as jnp
from jax import lax
from jax.experimental import pallas as pl
from jax.experimental.pallas import tpu as pltpu
from jax.sharding import PartitionSpec as P

HEAD_DIM = 128
SLOT = 6
LIVE = 120
EPS = 1e-05
SCALE = 1.0 / math.sqrt(HEAD_DIM)
F32 = jnp.float32
BF16 = jnp.bfloat16
NT = (((1,), (1,)), ((), ()))
TN = (((0,), (0,)), ((), ()))


def dot(a, b):
    return jnp.dot(a, b, preferred_element_type=F32)


def dot_nt(a, b):
    return lax.dot_general(a, b, NT, preferred_element_type=F32)


def dot_tn(a, b):
    return lax.dot_general(a, b, TN, preferred_element_type=F32)


def shift(block, axis, by):
    count = lax.axis_size(axis)
    return lax.ppermute(block, axis, [(i, (i + by) % count) for i in range(count)])


def widen(shard):
    me = lax.axis_index("mp")
    width = shard.shape[1]
    across = shift(shard, "mp", 2)
    right = shift(shard, "mp", 1)
    left = shift(shard, "mp", 3)
    full = jnp.zeros((shard.shape[0], 4 * width), shard.dtype)
    for block, by in ((shard, 0), (right, 3), (left, 1), (across, 2)):
        full = lax.dynamic_update_slice(full, block, (0, (me + by) % 4 * width))
    return full


def narrow(partial):
    me = lax.axis_index("mp")
    width = partial.shape[1] // 4

    def block(by):
        return lax.dynamic_slice(
            partial, (0, (me + by) % 4 * width), (partial.shape[0], width)
        )

    across = shift(block(2).astype(BF16), "mp", 2)
    right = shift(block(1).astype(BF16), "mp", 1)
    left = shift(block(3).astype(BF16), "mp", 3)
    return block(0) + right.astype(F32) + left.astype(F32) + across.astype(F32)


def partner(block):
    return lax.ppermute(block, "section", [(0, 1), (1, 0)])


def shift_part(block, stride, size, by):
    count = lax.axis_size("dp")
    route = []
    for i in range(count):
        part = i // stride % size
        route.append((i, i + ((part + by) % size - part) * stride))
    return lax.ppermute(block, "dp", route)


def other_core(block):
    return shift_part(block, 1, 2, 1)


def pick_kernel(core, a_ref, mine_ref, other_ref):
    for out_ref, which in ((mine_ref, core[0]), (other_ref, 1 - core[0])):
        for j in range(16):
            at = pl.multiple_of((j % 4 * 8 + j // 4 * 2 + which) * 128, 128)
            out_ref[:, j * 128 : (j + 1) * 128] = a_ref[:, pl.ds(at, 128)]


def pick(a, core):
    rows, cols = a.shape
    half = jax.ShapeDtypeStruct((rows, cols // 2), a.dtype)
    vmem = pl.BlockSpec(memory_space=pltpu.VMEM)
    return pl.pallas_call(
        pick_kernel,
        out_shape=(half, half),
        in_specs=[pl.BlockSpec(memory_space=pltpu.SMEM), vmem],
        out_specs=(vmem, vmem),
        cost_estimate=pl.CostEstimate(
            flops=rows * cols, bytes_accessed=4 * rows * cols, transcendentals=0
        ),
        name="pick",
    )(core.reshape(1), a)


def products(lefts, rights):
    return sum(dot_tn(left, right) for left, right in zip(lefts, rights))


def sum_along(total, at, stride, axis):
    def part(by):
        return lax.dynamic_index_in_dim(total, (at + by) % 4, axis, keepdims=False)

    held = part(0).astype(F32)
    for by in (2, 1, 3):
        held = held + shift_part(part(by).astype(BF16), stride, 4, by).astype(F32)
    return held


def sum_over_y(total, axis=0):
    return sum_along(total, lax.axis_index("dp") // 2, 2, axis)


def sum_over_z(total, axis=0):
    return sum_along(total, lax.axis_index("dp") // 8, 8, axis)


def sum_over_z_at_once(total):
    count = lax.axis_size("dp")
    parts = lax.all_to_all(
        total.transpose(1, 0, 2, 3),
        "dp",
        split_axis=0,
        concat_axis=0,
        tiled=True,
        axis_index_groups=[[z * 8 + i for z in range(count // 8)] for i in range(8)],
    )
    return jnp.sum(parts.astype(F32), axis=0)


def attend(full, w_query, w_key, w_value, allowed):
    wide = full.astype(F32)
    inv_rms = lax.rsqrt(jnp.mean(wide * wide, axis=1, keepdims=True) + EPS)
    normed = (wide * inv_rms).astype(BF16)
    query = dot(normed, w_query).astype(BF16)
    key = dot(normed, w_key).astype(BF16)
    value = dot(normed, w_value).astype(BF16)
    heads = query.reshape(query.shape[0], -1, HEAD_DIM)
    scores = jnp.einsum("qrd,kd->rqk", heads, key, preferred_element_type=F32) * SCALE
    raised = jnp.exp(jnp.where(allowed, scores, -jnp.inf))
    probs = raised / jnp.sum(raised, axis=2, keepdims=True)
    probs_low = probs.astype(BF16)
    attended = jnp.einsum("rqk,kd->qrd", probs_low, value, preferred_element_type=F32)
    attended = attended.reshape(query.shape).astype(BF16)
    return dict(
        full=full,
        inv_rms=inv_rms,
        normed=normed,
        heads=heads,
        key=key,
        value=value,
        probs=probs,
        probs_low=probs_low,
        attended=attended,
    )


def attend_back(grad_full, w_out, saved):
    rows = grad_full.shape[0]
    probs, key, value, heads = saved["probs"], saved["key"], saved["value"], saved["heads"]
    d_heads = dot_nt(grad_full, w_out).astype(BF16).reshape(heads.shape)
    d_value = jnp.einsum("rqk,qrd->kd", saved["probs_low"], d_heads, preferred_element_type=F32)
    d_value = d_value.astype(BF16)
    d_probs = jnp.einsum("qrd,kd->rqk", d_heads, value, preferred_element_type=F32)
    d_scores = probs * (d_probs - jnp.sum(probs * d_probs, axis=2, keepdims=True)) * SCALE
    d_scores = d_scores.astype(BF16)
    d_query = jnp.einsum("rqk,kd->qrd", d_scores, key, preferred_element_type=F32)
    d_query = d_query.reshape(rows, -1).astype(BF16)
    d_key = jnp.einsum("rqk,qrd->kd", d_scores, heads, preferred_element_type=F32).astype(BF16)
    return d_query, d_key, d_value


def norm_back(d_cols, w_query, w_key, w_value, saved):
    d_query, d_key, d_value = d_cols
    d_normed = dot_nt(d_query, w_query) + dot_nt(d_key, w_key) + dot_nt(d_value, w_value)
    wide = saved["full"].astype(F32) * saved["inv_rms"]
    return saved["inv_rms"] * (
        d_normed - wide * jnp.mean(d_normed * wide, axis=1, keepdims=True)
    )


def on_device(embeds, lengths, owners, w_query, w_key, w_value, w_out, cycle_grad):
    pairs = lax.axis_size("dp")
    dp_self = lax.axis_index("dp")
    core = dp_self % 2
    rows, width = embeds.shape[1:]
    w_query, w_key, w_value, w_out = w_query[0], w_key[0], w_value[0], w_out[0]

    own_len = lax.dynamic_slice_in_dim(lengths, dp_self, 1, 0)[0]
    own_owner = lax.dynamic_slice_in_dim(owners, dp_self, 1, 0)[0]
    slots = jnp.arange(pairs, dtype=jnp.int32)
    ends = jnp.sum(jnp.where(slots[None, :] <= slots[:, None], own_len[None, :], 0), axis=1)
    starts = ends - own_len
    live_ids = jnp.arange(LIVE, dtype=jnp.int32)
    in_slot = (live_ids[:, None] >= starts[None, :]) & (live_ids[:, None] < ends[None, :])

    def of_slot(table):
        return jnp.sum(jnp.where(in_slot, table[None, :], 0), axis=1)

    slot = of_slot(slots)
    place = live_ids - of_slot(starts)
    at_source = slot * SLOT + place
    at_owner = of_slot(own_owner) * SLOT + place
    row_ids = jnp.arange(rows, dtype=jnp.int32)
    from_source = (at_source[:, None] == row_ids[None, :]).astype(BF16)
    from_owner = (at_owner[:, None] == row_ids[None, :]).astype(BF16)
    allowed = (slot[:, None] == slot[None, :]) & (live_ids[None, :] <= live_ids[:, None])

    def regroup(block):
        split = block.reshape(pairs, SLOT, width)
        return lax.all_to_all(split, "dp", split_axis=0, concat_axis=0, tiled=True).reshape(
            rows, width
        )

    barrier = lax.optimization_barrier
    wq, wk = w_query.shape[1], w_key.shape[1]

    def left_pair(left):
        mine, other = pick(left, core)
        return [mine, other_core(other)]

    def right_pair(right):
        return [right, other_core(right)]

    def by_owner(total):
        return total.astype(BF16).reshape(4, 4, 128, -1)

    grad_rows = regroup(cycle_grad[0])
    moved = dot(from_source, embeds[0]).astype(BF16)
    moved_full = widen(moved)
    first = attend(moved_full, w_query, w_key, w_value, allowed)
    norm_first = left_pair(first["normed"])
    att_first = right_pair(first["attended"])
    branch = narrow(dot(first["attended"], w_out))
    decoded = (moved.astype(F32) + branch).astype(BF16)
    grad = dot(from_owner, grad_rows).astype(BF16)
    decoded, grad, norm_first, att_first = barrier((decoded, grad, norm_first, att_first))
    incoming = partner(decoded)
    grad_full = lax.all_gather(grad, "mp", axis=1, tiled=True)
    incoming, grad_full = barrier((incoming, grad_full))
    incoming_full = widen(incoming)
    grad_left = left_pair(grad_full)
    incoming_full, grad_left = barrier((incoming_full, grad_left))
    second = attend(incoming_full, w_query, w_key, w_value, allowed)
    cols_second = attend_back(grad_full, w_out, second)
    d_second = norm_back(cols_second, w_query, w_key, w_value, second)
    norm_second = left_pair(second["normed"])
    att_second = right_pair(second["attended"])
    right_second = right_pair(jnp.concatenate(cols_second, axis=1))
    back = (grad.astype(F32) + narrow(d_second)).astype(BF16)
    back, norm_second, att_second, right_second = barrier(
        (back, norm_second, att_second, right_second)
    )
    ret = partner(back)
    out_base = products(grad_left, att_second)
    ret, out_base = barrier((ret, out_base))
    ret_full = widen(ret)
    q_base = products(norm_second, [right[:, :wq] for right in right_second])
    kv_base = products(norm_second, [right[:, wq:] for right in right_second])
    ret_full, q_base, kv_base = barrier((ret_full, q_base, kv_base))
    ret_left = left_pair(ret_full)
    cols_first = attend_back(ret_full, w_out, first)
    out_part = by_owner(out_base + products(ret_left, att_first))
    out_part, cols_first = barrier((out_part, cols_first))
    right_first = right_pair(jnp.concatenate(cols_first, axis=1))
    q_part = by_owner(q_base + products(norm_first, [right[:, :wq] for right in right_first]))
    kv_part = by_owner(kv_base + products(norm_first, [right[:, wq:] for right in right_first]))
    q_part, kv_part, cols_first = barrier((q_part, kv_part, cols_first))
    kv_sum = sum_over_z_at_once(kv_part)
    d_first = norm_back(cols_first, w_query, w_key, w_value, first)
    out_sum = sum_over_y(out_part)
    d_first, late, out_sum = barrier((d_first, second["attended"], out_sum))
    out_sum = sum_over_z(out_sum.reshape(4, 128, -1))
    q_sum = sum_over_z(sum_over_y(q_part).reshape(4, 128, -1))
    cycled = (incoming.astype(F32) + narrow(dot(late, w_out))).astype(BF16)
    kv_sum, cycled = barrier((kv_sum, cycled))
    kv_sum = sum_over_y(kv_sum.reshape(4, 128, -1))
    cycled_rows = regroup(dot_tn(from_owner, cycled).astype(BF16))
    front = (ret.astype(F32) + narrow(d_first)).astype(BF16)
    restored = dot_tn(from_source, front).astype(BF16)
    return (
        cycled_rows[None],
        restored[None],
        q_sum[None],
        kv_sum[None, :, :wk],
        kv_sum[None, :, wk:],
        out_sum[None],
    )


def solution(mesh):
    rows = P("section", "dp", "mp")
    columns = P("section", None, "mp")
    return jax.shard_map(
        on_device,
        mesh=mesh,
        in_specs=(rows, P(), P(), columns, columns, columns, P("section", "mp", None), rows),
        out_specs=(rows,) * 6,
        check_vma=False,
    )
```

```python
import math

import jax
import jax.numpy as jnp
from jax import lax
from jax.sharding import PartitionSpec as P

HEAD_DIM = 128
SLOT = 6
LIVE = 120
EPS = 1e-05
SCALE = 1.0 / math.sqrt(HEAD_DIM)
F32 = jnp.float32
BF16 = jnp.bfloat16
NT = (((1,), (1,)), ((), ()))
TN = (((0,), (0,)), ((), ()))


def dot(a, b):
    return jnp.dot(a, b, preferred_element_type=F32)


def dot_nt(a, b):
    return lax.dot_general(a, b, NT, preferred_element_type=F32)


def dot_tn(a, b):
    return lax.dot_general(a, b, TN, preferred_element_type=F32)


def shift(block, axis, by):
    count = lax.axis_size(axis)
    return lax.ppermute(block, axis, [(i, (i + by) % count) for i in range(count)])


def widen(shard, behind=None):
    me = lax.axis_index("mp")
    width = shard.shape[1]
    across = shift(shard, "mp", 2)
    right = shift(shard, "mp", 1)
    left = shift(shard, "mp", 3)
    if behind is not None:
        right, behind = lax.optimization_barrier((right, behind))
    full = jnp.zeros((shard.shape[0], 4 * width), shard.dtype)
    for block, by in ((shard, 0), (right, 3), (left, 1), (across, 2)):
        full = lax.dynamic_update_slice(full, block, (0, (me + by) % 4 * width))
    return full if behind is None else (full, behind)


def narrow(partial):
    me = lax.axis_index("mp")
    width = partial.shape[1] // 4

    def block(by):
        return lax.dynamic_slice(
            partial, (0, (me + by) % 4 * width), (partial.shape[0], width)
        )

    across = shift(block(2).astype(BF16), "mp", 2)
    right = shift(block(1).astype(BF16), "mp", 1)
    left = shift(block(3).astype(BF16), "mp", 3)
    return block(0) + right.astype(F32) + left.astype(F32) + across.astype(F32)


def partner(block):
    return lax.ppermute(block, "section", [(0, 1), (1, 0)])


def shift_part(block, stride, size, by):
    count = lax.axis_size("dp")
    route = []
    for i in range(count):
        part = i // stride % size
        route.append((i, i + ((part + by) % size - part) * stride))
    return lax.ppermute(block, "dp", route)


def other_core(block):
    return shift_part(block, 1, 2, 1)


def stack(blocks):
    rows, cols = blocks[0].shape
    held = jnp.zeros((len(blocks) * rows, cols), blocks[0].dtype)
    for k, block in enumerate(blocks):
        held = lax.dynamic_update_slice(held, block, (k * rows, 0))
    return held


def pick(blocks, at, axis):
    return lax.dynamic_index_in_dim(blocks, at, axis, keepdims=False)


def sum_over_core(total):
    core = lax.axis_index("dp") % 2
    parts = total.reshape(4, 4, 2, 128, -1)
    return pick(parts, core, 2).astype(F32) + other_core(pick(parts, 1 - core, 2)).astype(F32)


def sum_over_four(total, at, stride, axis, behind=()):
    held = pick(total, at % 4, axis)
    for by in (1, 3, 2):
        part = pick(total, (at + by) % 4, axis)
        came = shift_part(part.astype(BF16), stride, 4, by)
        if by == 1 and behind:
            came, *behind = lax.optimization_barrier((came, *behind))
        held = held + came.astype(F32)
    return (held, *behind) if behind else held


def sum_over_y(total, axis, behind=()):
    return sum_over_four(total, lax.axis_index("dp") // 2, 2, axis, behind)


def sum_over_z(total, axis):
    return sum_over_four(total, lax.axis_index("dp") // 8, 8, axis)


def sum_over_z_by_halves(total):
    z = lax.axis_index("dp") // 8
    parts = total.reshape((2, 2) + total.shape[1:])
    sent = pick(parts, 1 - z % 2, 1).astype(BF16)
    held = pick(parts, z % 2, 1) + shift_part(sent, 8, 2, 1).astype(F32)
    sent = pick(held, 1 - z // 2, 0).astype(BF16)
    return pick(held, z // 2, 0) + shift_part(sent, 16, 2, 1).astype(F32)


def narrow_at_once(partials):
    rows = jnp.concatenate([p.astype(BF16).reshape(LIVE, 4, -1) for p in partials], axis=0)
    parts = lax.all_to_all(
        rows.transpose(1, 0, 2), "mp", split_axis=0, concat_axis=0, tiled=True
    )
    total = jnp.sum(parts.astype(F32), axis=0)
    return [total[k * LIVE : (k + 1) * LIVE] for k in range(len(partials))]


def attend(full, w_query, w_key, w_value, allowed):
    wide = full.astype(F32)
    inv_rms = lax.rsqrt(jnp.mean(wide * wide, axis=1, keepdims=True) + EPS)
    normed = (wide * inv_rms).astype(BF16)
    query = dot(normed, w_query).astype(BF16)
    key = dot(normed, w_key).astype(BF16)
    value = dot(normed, w_value).astype(BF16)
    heads = query.reshape(query.shape[0], -1, HEAD_DIM)
    scores = jnp.einsum("qrd,kd->rqk", heads, key, preferred_element_type=F32) * SCALE
    raised = jnp.exp(jnp.where(allowed, scores, -jnp.inf))
    probs = raised / jnp.sum(raised, axis=2, keepdims=True)
    probs_low = probs.astype(BF16)
    attended = jnp.einsum("rqk,kd->qrd", probs_low, value, preferred_element_type=F32)
    attended = attended.reshape(query.shape).astype(BF16)
    return dict(
        full=full,
        inv_rms=inv_rms,
        normed=normed,
        heads=heads,
        key=key,
        value=value,
        probs=probs,
        probs_low=probs_low,
        attended=attended,
    )


def attend_back(grad_full, w_out, saved):
    rows = grad_full.shape[0]
    probs, key, value, heads = saved["probs"], saved["key"], saved["value"], saved["heads"]
    d_heads = dot_nt(grad_full, w_out).astype(BF16).reshape(heads.shape)
    d_value = jnp.einsum("rqk,qrd->kd", saved["probs_low"], d_heads, preferred_element_type=F32)
    d_value = d_value.astype(BF16)
    d_probs = jnp.einsum("qrd,kd->rqk", d_heads, value, preferred_element_type=F32)
    d_scores = probs * (d_probs - jnp.sum(probs * d_probs, axis=2, keepdims=True)) * SCALE
    d_scores = d_scores.astype(BF16)
    d_query = jnp.einsum("rqk,kd->qrd", d_scores, key, preferred_element_type=F32)
    d_query = d_query.reshape(rows, -1).astype(BF16)
    d_key = jnp.einsum("rqk,qrd->kd", d_scores, heads, preferred_element_type=F32).astype(BF16)
    return d_query, d_key, d_value


def norm_back(d_cols, w_query, w_key, w_value, saved):
    d_query, d_key, d_value = d_cols
    d_normed = dot_nt(d_query, w_query) + dot_nt(d_key, w_key) + dot_nt(d_value, w_value)
    wide = saved["full"].astype(F32) * saved["inv_rms"]
    return saved["inv_rms"] * (
        d_normed - wide * jnp.mean(d_normed * wide, axis=1, keepdims=True)
    )


def on_device(embeds, lengths, owners, w_query, w_key, w_value, w_out, cycle_grad):
    pairs = lax.axis_size("dp")
    dp_self = lax.axis_index("dp")
    rows, width = embeds.shape[1:]
    w_query, w_key, w_value, w_out = w_query[0], w_key[0], w_value[0], w_out[0]

    own_len = lax.dynamic_slice_in_dim(lengths, dp_self, 1, 0)[0]
    own_owner = lax.dynamic_slice_in_dim(owners, dp_self, 1, 0)[0]
    slots = jnp.arange(pairs, dtype=jnp.int32)
    ends = jnp.sum(jnp.where(slots[None, :] <= slots[:, None], own_len[None, :], 0), axis=1)
    starts = ends - own_len
    live_ids = jnp.arange(LIVE, dtype=jnp.int32)
    in_slot = (live_ids[:, None] >= starts[None, :]) & (live_ids[:, None] < ends[None, :])

    def of_slot(table):
        return jnp.sum(jnp.where(in_slot, table[None, :], 0), axis=1)

    slot = of_slot(slots)
    place = live_ids - of_slot(starts)
    at_source = slot * SLOT + place
    at_owner = of_slot(own_owner) * SLOT + place
    row_ids = jnp.arange(rows, dtype=jnp.int32)
    from_source = (at_source[:, None] == row_ids[None, :]).astype(BF16)
    from_owner = (at_owner[:, None] == row_ids[None, :]).astype(BF16)
    allowed = (slot[:, None] == slot[None, :]) & (live_ids[None, :] <= live_ids[:, None])

    def regroup(block):
        split = block.reshape(pairs, SLOT, width)
        return lax.all_to_all(split, "dp", split_axis=0, concat_axis=0, tiled=True).reshape(
            rows, width
        )

    barrier = lax.optimization_barrier
    wq, wk = w_query.shape[1], w_key.shape[1]
    grad_rows = regroup(cycle_grad[0])
    moved = dot(from_source, embeds[0]).astype(BF16)
    moved_full = widen(moved)
    first = attend(moved_full, w_query, w_key, w_value, allowed)
    branch = narrow(dot(first["attended"], w_out))
    decoded = (moved.astype(F32) + branch).astype(BF16)
    grad = dot(from_owner, grad_rows).astype(BF16)
    decoded, grad = barrier((decoded, grad))
    incoming = partner(decoded)
    incoming_full, grad = widen(incoming, grad)
    grad_full = widen(grad)
    second = attend(incoming_full, w_query, w_key, w_value, allowed)
    cols_second = attend_back(grad_full, w_out, second)
    d_second = norm_back(cols_second, w_query, w_key, w_value, second)
    back = (grad.astype(F32) + narrow(d_second)).astype(BF16)
    ret = partner(back)
    norm = stack([second["normed"], first["normed"]])
    att = stack([second["attended"], first["attended"]])
    ret, norm, att = barrier((ret, norm, att))
    ret_full = widen(ret)
    cols_first = attend_back(ret_full, w_out, first)
    out_part = dot_tn(stack([grad_full, ret_full]), att).astype(BF16)
    out_part, cols_first = barrier((out_part, cols_first))
    cols = stack([jnp.concatenate(cols_second, axis=1), jnp.concatenate(cols_first, axis=1)])
    qkv_part = dot_tn(norm, cols).astype(BF16)
    out_sum = sum_over_core(out_part)
    out_sum, qkv_part = barrier((out_sum, qkv_part))
    out_sum = sum_over_y(out_sum, 1)
    qkv_sum = sum_over_core(qkv_part)
    qkv_sum, cols_first = barrier((qkv_sum, cols_first))
    d_first = norm_back(cols_first, w_query, w_key, w_value, first)
    qkv_sum, d_first, late = sum_over_y(qkv_sum, 1, (d_first, second["attended"]))
    out_sum = sum_over_z_by_halves(out_sum)
    qkv_sum = sum_over_z(qkv_sum, 0)
    d_total, branch = narrow_at_once([d_first, dot(late, w_out)])
    cycled = (incoming.astype(F32) + branch).astype(BF16)
    cycled_rows = regroup(dot_tn(from_owner, cycled).astype(BF16))
    front = (ret.astype(F32) + d_total).astype(BF16)
    restored = dot_tn(from_source, front).astype(BF16)
    return (
        cycled_rows[None],
        restored[None],
        qkv_sum[None, :, :wq],
        qkv_sum[None, :, wq : wq + wk],
        qkv_sum[None, :, wq + wk :],
        out_sum[None],
    )


def solution(mesh):
    rows = P("section", "dp", "mp")
    columns = P("section", None, "mp")
    return jax.shard_map(
        on_device,
        mesh=mesh,
        in_specs=(rows, P(), P(), columns, columns, columns, P("section", "mp", None), rows),
        out_specs=(rows,) * 6,
        check_vma=False,
    )
```

```python
import math

import jax
import jax.numpy as jnp
from jax import lax
from jax.sharding import PartitionSpec as P

HEAD_DIM = 128
SLOT = 6
LIVE = 120
EPS = 1e-05
SCALE = 1.0 / math.sqrt(HEAD_DIM)
F32 = jnp.float32
BF16 = jnp.bfloat16
NT = (((1,), (1,)), ((), ()))
TN = (((0,), (0,)), ((), ()))


def dot(a, b):
    return jnp.dot(a, b, preferred_element_type=F32)


def dot_nt(a, b):
    return lax.dot_general(a, b, NT, preferred_element_type=F32)


def dot_tn(a, b):
    return lax.dot_general(a, b, TN, preferred_element_type=F32)


def shift(block, axis, by):
    count = lax.axis_size(axis)
    return lax.ppermute(block, axis, [(i, (i + by) % count) for i in range(count)])


def widen(shard, behind=None):
    me = lax.axis_index("mp")
    width = shard.shape[1]
    across = shift(shard, "mp", 2)
    right = shift(shard, "mp", 1)
    left = shift(shard, "mp", 3)
    if behind is not None:
        right, behind = lax.optimization_barrier((right, behind))
    full = jnp.zeros((shard.shape[0], 4 * width), shard.dtype)
    for block, by in ((shard, 0), (right, 3), (left, 1), (across, 2)):
        full = lax.dynamic_update_slice(full, block, (0, (me + by) % 4 * width))
    return full if behind is None else (full, behind)


def narrow(partial):
    me = lax.axis_index("mp")
    width = partial.shape[1] // 4

    def block(by):
        return lax.dynamic_slice(
            partial, (0, (me + by) % 4 * width), (partial.shape[0], width)
        )

    across = shift(block(2).astype(BF16), "mp", 2)
    right = shift(block(1).astype(BF16), "mp", 1)
    left = shift(block(3).astype(BF16), "mp", 3)
    return block(0).astype(F32) + right.astype(F32) + left.astype(F32) + across.astype(F32)


def partner(block):
    return lax.ppermute(block, "section", [(0, 1), (1, 0)])


def shift_part(block, stride, size, by):
    count = lax.axis_size("dp")
    route = []
    for i in range(count):
        part = i // stride % size
        route.append((i, i + ((part + by) % size - part) * stride))
    return lax.ppermute(block, "dp", route)


def other_core(block):
    return shift_part(block, 1, 2, 1)


def stack(blocks):
    rows, cols = blocks[0].shape
    held = jnp.zeros((len(blocks) * rows, cols), blocks[0].dtype)
    for k, block in enumerate(blocks):
        held = lax.dynamic_update_slice(held, block, (k * rows, 0))
    return held


def pick(blocks, at, axis):
    return lax.dynamic_index_in_dim(blocks, at, axis, keepdims=False)


def sum_over_core(total):
    core = lax.axis_index("dp") % 2
    parts = total.reshape(4, 4, 2, 128, -1)
    came = other_core(pick(parts, 1 - core, 2))
    return (pick(parts, core, 2).astype(F32) + came.astype(F32)).astype(BF16)


def sum_over_four(total, at, stride, axis):
    held = pick(total, at % 4, axis).astype(F32)
    for by in (2, 1, 3):
        part = pick(total, (at + by) % 4, axis)
        held = held + shift_part(part.astype(BF16), stride, 4, by).astype(F32)
    return held


def sum_over_y(total, axis):
    return sum_over_four(total, lax.axis_index("dp") // 2, 2, axis)


def sum_over_z(total, axis):
    return sum_over_four(total, lax.axis_index("dp") // 8, 8, axis)


def attend(full, w_query, w_key, w_value, allowed):
    wide = full.astype(F32)
    inv_rms = lax.rsqrt(jnp.mean(wide * wide, axis=1, keepdims=True) + EPS)
    normed = (wide * inv_rms).astype(BF16)
    query = dot(normed, w_query).astype(BF16)
    key = dot(normed, w_key).astype(BF16)
    value = dot(normed, w_value).astype(BF16)
    heads = query.reshape(query.shape[0], -1, HEAD_DIM)
    scores = jnp.einsum("qrd,kd->rqk", heads, key, preferred_element_type=F32) * SCALE
    raised = jnp.exp(jnp.where(allowed, scores, -jnp.inf))
    probs = raised / jnp.sum(raised, axis=2, keepdims=True)
    probs_low = probs.astype(BF16)
    attended = jnp.einsum("rqk,kd->qrd", probs_low, value, preferred_element_type=F32)
    attended = attended.reshape(query.shape).astype(BF16)
    return dict(
        full=full,
        inv_rms=inv_rms,
        normed=normed,
        heads=heads,
        key=key,
        value=value,
        probs=probs,
        probs_low=probs_low,
        attended=attended,
    )


def attend_back(grad_full, w_out, saved):
    rows = grad_full.shape[0]
    probs, key, value, heads = saved["probs"], saved["key"], saved["value"], saved["heads"]
    d_heads = dot_nt(grad_full, w_out).astype(BF16).reshape(heads.shape)
    d_value = jnp.einsum("rqk,qrd->kd", saved["probs_low"], d_heads, preferred_element_type=F32)
    d_value = d_value.astype(BF16)
    d_probs = jnp.einsum("qrd,kd->rqk", d_heads, value, preferred_element_type=F32)
    d_scores = probs * (d_probs - jnp.sum(probs * d_probs, axis=2, keepdims=True)) * SCALE
    d_scores = d_scores.astype(BF16)
    d_query = jnp.einsum("rqk,kd->qrd", d_scores, key, preferred_element_type=F32)
    d_query = d_query.reshape(rows, -1).astype(BF16)
    d_key = jnp.einsum("rqk,qrd->kd", d_scores, heads, preferred_element_type=F32).astype(BF16)
    return d_query, d_key, d_value


def norm_back(d_cols, w_query, w_key, w_value, saved):
    d_query, d_key, d_value = d_cols
    d_normed = dot_nt(d_query, w_query) + dot_nt(d_key, w_key) + dot_nt(d_value, w_value)
    wide = saved["full"].astype(F32) * saved["inv_rms"]
    return saved["inv_rms"] * (
        d_normed - wide * jnp.mean(d_normed * wide, axis=1, keepdims=True)
    )


def on_device(embeds, lengths, owners, w_query, w_key, w_value, w_out, cycle_grad):
    pairs = lax.axis_size("dp")
    dp_self = lax.axis_index("dp")
    rows, width = embeds.shape[1:]
    w_query, w_key, w_value, w_out = w_query[0], w_key[0], w_value[0], w_out[0]

    own_len = lax.dynamic_slice_in_dim(lengths, dp_self, 1, 0)[0]
    own_owner = lax.dynamic_slice_in_dim(owners, dp_self, 1, 0)[0]
    slots = jnp.arange(pairs, dtype=jnp.int32)
    ends = jnp.sum(jnp.where(slots[None, :] <= slots[:, None], own_len[None, :], 0), axis=1)
    starts = ends - own_len
    live_ids = jnp.arange(LIVE, dtype=jnp.int32)
    in_slot = (live_ids[:, None] >= starts[None, :]) & (live_ids[:, None] < ends[None, :])

    def of_slot(table):
        return jnp.sum(jnp.where(in_slot, table[None, :], 0), axis=1)

    slot = of_slot(slots)
    place = live_ids - of_slot(starts)
    at_source = slot * SLOT + place
    at_owner = of_slot(own_owner) * SLOT + place
    row_ids = jnp.arange(rows, dtype=jnp.int32)
    from_source = (at_source[:, None] == row_ids[None, :]).astype(BF16)
    from_owner = (at_owner[:, None] == row_ids[None, :]).astype(BF16)
    allowed = (slot[:, None] == slot[None, :]) & (live_ids[None, :] <= live_ids[:, None])

    def regroup(block):
        split = block.reshape(pairs, SLOT, width)
        return lax.all_to_all(split, "dp", split_axis=0, concat_axis=0, tiled=True).reshape(
            rows, width
        )

    barrier = lax.optimization_barrier
    wq, wk = w_query.shape[1], w_key.shape[1]
    grad_rows = regroup(cycle_grad[0])
    moved = dot(from_source, embeds[0]).astype(BF16)
    moved_full = widen(moved)
    first = attend(moved_full, w_query, w_key, w_value, allowed)
    branch = narrow(dot(first["attended"], w_out))
    decoded = (moved.astype(F32) + branch).astype(BF16)
    grad = dot(from_owner, grad_rows).astype(BF16)
    decoded, grad = barrier((decoded, grad))
    incoming = partner(decoded)
    incoming_full, grad = widen(incoming, grad)
    grad_full = widen(grad)
    second = attend(incoming_full, w_query, w_key, w_value, allowed)
    cols_second = attend_back(grad_full, w_out, second)
    d_second = norm_back(cols_second, w_query, w_key, w_value, second)
    back = (grad.astype(F32) + narrow(d_second)).astype(BF16)
    branch = dot(second["attended"], w_out).astype(BF16)
    norm = stack([second["normed"], first["normed"]])
    att = stack([second["attended"], first["attended"]])
    back, branch, norm, att = barrier((back, branch, norm, att))
    ret = partner(back)
    ret_full, branch = widen(ret, branch)
    cycled = (incoming.astype(F32) + narrow(branch)).astype(BF16)
    cols_first = attend_back(ret_full, w_out, first)
    out_part = dot_tn(stack([grad_full, ret_full]), att).astype(BF16)
    out_part, cols_first, cycled = barrier((out_part, cols_first, cycled))
    cols = stack([jnp.concatenate(cols_second, axis=1), jnp.concatenate(cols_first, axis=1)])
    qkv_part = dot_tn(norm, cols).astype(BF16)
    out_sum = sum_over_core(out_part)
    qkv_sum = sum_over_core(qkv_part)
    out_sum, qkv_sum, cols_first = barrier((out_sum, qkv_sum, cols_first))
    out_sum = sum_over_y(out_sum, 1)
    qkv_sum = sum_over_y(qkv_sum, 1)
    d_first = norm_back(cols_first, w_query, w_key, w_value, first)
    d_first, cycled = barrier((d_first, cycled))
    cycled_rows = regroup(dot_tn(from_owner, cycled).astype(BF16))
    out_sum, d_first, cycled_rows = barrier((out_sum, d_first, cycled_rows))
    out_sum = sum_over_z(out_sum, 0)
    qkv_sum = sum_over_z(qkv_sum, 0)
    front = (ret.astype(F32) + narrow(d_first)).astype(BF16)
    restored = dot_tn(from_source, front).astype(BF16)
    return (
        cycled_rows[None],
        restored[None],
        qkv_sum[None, :, :wq],
        qkv_sum[None, :, wq : wq + wk],
        qkv_sum[None, :, wq + wk :],
        out_sum[None],
    )


def solution(mesh):
    rows = P("section", "dp", "mp")
    columns = P("section", None, "mp")
    return jax.shard_map(
        on_device,
        mesh=mesh,
        in_specs=(rows, P(), P(), columns, columns, columns, P("section", "mp", None), rows),
        out_specs=(rows,) * 6,
        check_vma=False,
    )
```

```python
import math

import jax
import jax.numpy as jnp
from jax import lax
from jax.experimental import pallas as pl
from jax.experimental.pallas import tpu as pltpu
from jax.sharding import PartitionSpec as P

HEAD_DIM = 128
SLOT = 6
LIVE = 120
EPS = 1e-05
SCALE = 1.0 / math.sqrt(HEAD_DIM)
F32 = jnp.float32
BF16 = jnp.bfloat16
NT = (((1,), (1,)), ((), ()))
TN = (((0,), (0,)), ((), ()))


def dot(a, b):
    return jnp.dot(a, b, preferred_element_type=F32)


def dot_nt(a, b):
    return lax.dot_general(a, b, NT, preferred_element_type=F32)


def dot_tn(a, b):
    return lax.dot_general(a, b, TN, preferred_element_type=F32)


def shift(block, axis, by):
    count = lax.axis_size(axis)
    return lax.ppermute(block, axis, [(i, (i + by) % count) for i in range(count)])


def widen(shard, behind=None):
    me = lax.axis_index("mp")
    width = shard.shape[1]
    across = shift(shard, "mp", 2)
    right = shift(shard, "mp", 1)
    left = shift(shard, "mp", 3)
    if behind is not None:
        right, behind = lax.optimization_barrier((right, behind))
    full = jnp.zeros((shard.shape[0], 4 * width), shard.dtype)
    for block, by in ((shard, 0), (right, 3), (left, 1), (across, 2)):
        full = lax.dynamic_update_slice(full, block, (0, (me + by) % 4 * width))
    return full if behind is None else (full, behind)


def narrow(partial, behind=None):
    me = lax.axis_index("mp")
    width = partial.shape[1] // 4

    def block(by):
        return lax.dynamic_slice(
            partial, (0, (me + by) % 4 * width), (partial.shape[0], width)
        )

    across = shift(block(2).astype(BF16), "mp", 2)
    right = shift(block(1).astype(BF16), "mp", 1)
    left = shift(block(3).astype(BF16), "mp", 3)
    if behind is not None:
        right, behind = lax.optimization_barrier((right, behind))
    total = block(0).astype(F32) + right.astype(F32) + left.astype(F32) + across.astype(F32)
    return total if behind is None else (total, behind)


def partner(block):
    return lax.ppermute(block, "section", [(0, 1), (1, 0)])


def shift_part(block, stride, size, by):
    count = lax.axis_size("dp")
    route = []
    for i in range(count):
        part = i // stride % size
        route.append((i, i + ((part + by) % size - part) * stride))
    return lax.ppermute(block, "dp", route)


def other_core(block):
    return shift_part(block, 1, 2, 1)


def stack(blocks):
    rows, cols = blocks[0].shape
    held = jnp.zeros((len(blocks) * rows, cols), blocks[0].dtype)
    for k, block in enumerate(blocks):
        held = lax.dynamic_update_slice(held, block, (k * rows, 0))
    return held


def pick(blocks, at, axis):
    return lax.dynamic_index_in_dim(blocks, at, axis, keepdims=False)


def split_kernel(core, a_ref, mine_ref, other_ref):
    for out_ref, which in ((mine_ref, core[0]), (other_ref, 1 - core[0])):
        for j in range(16):
            at = pl.multiple_of((2 * j + which) * 128, 128)
            out_ref[:, j * 128 : (j + 1) * 128] = a_ref[:, pl.ds(at, 128)]


def split_by_core(a):
    rows, cols = a.shape
    half = jax.ShapeDtypeStruct((rows, cols // 2), a.dtype)
    vmem = pl.BlockSpec(memory_space=pltpu.VMEM)
    core = lax.axis_index("dp") % 2
    return pl.pallas_call(
        split_kernel,
        out_shape=(half, half),
        in_specs=[pl.BlockSpec(memory_space=pltpu.SMEM), vmem],
        out_specs=(vmem, vmem),
        cost_estimate=pl.CostEstimate(
            flops=rows * cols, bytes_accessed=4 * rows * cols, transcendentals=0
        ),
        name="split_by_core",
    )(core.reshape(1), a)


def product_over_core(mine, other, right):
    came = other_core(dot_tn(other, right).astype(BF16))
    total = (dot_tn(mine, right) + came.astype(F32)).astype(BF16)
    return total.reshape(4, 4, 128, -1)


def sum_over_four(total, at, stride, axis, own=None, ahead=()):
    came = [
        shift_part(pick(total, (at + by) % 4, axis).astype(BF16), stride, 4, by)
        for by in (2, 1, 3)
    ]
    came, ahead = lax.optimization_barrier((came, ahead))
    held = pick(total if own is None else own, at % 4, axis).astype(F32)
    for block in came:
        held = held + block.astype(F32)
    return (held, *ahead) if ahead else held


def sum_over_y(total, axis, own=None, ahead=()):
    return sum_over_four(total, lax.axis_index("dp") // 2, 2, axis, own, ahead)


def sum_over_z(total, axis):
    return sum_over_four(total, lax.axis_index("dp") // 8, 8, axis)


def attend(full, w_query, w_key, w_value, allowed):
    wide = full.astype(F32)
    inv_rms = lax.rsqrt(jnp.mean(wide * wide, axis=1, keepdims=True) + EPS)
    normed = (wide * inv_rms).astype(BF16)
    query = dot(normed, w_query).astype(BF16)
    key = dot(normed, w_key).astype(BF16)
    value = dot(normed, w_value).astype(BF16)
    heads = query.reshape(query.shape[0], -1, HEAD_DIM)
    scores = jnp.einsum("qrd,kd->rqk", heads, key, preferred_element_type=F32) * SCALE
    raised = jnp.exp(jnp.where(allowed, scores, -jnp.inf))
    probs = raised / jnp.sum(raised, axis=2, keepdims=True)
    probs_low = probs.astype(BF16)
    attended = jnp.einsum("rqk,kd->qrd", probs_low, value, preferred_element_type=F32)
    attended = attended.reshape(query.shape).astype(BF16)
    return dict(
        full=full,
        inv_rms=inv_rms,
        normed=normed,
        heads=heads,
        key=key,
        value=value,
        probs=probs,
        probs_low=probs_low,
        attended=attended,
    )


def attend_back(d_attended, saved):
    rows = d_attended.shape[0]
    probs, key, value, heads = saved["probs"], saved["key"], saved["value"], saved["heads"]
    d_heads = d_attended.reshape(heads.shape)
    d_value = jnp.einsum("rqk,qrd->kd", saved["probs_low"], d_heads, preferred_element_type=F32)
    d_value = d_value.astype(BF16)
    d_probs = jnp.einsum("qrd,kd->rqk", d_heads, value, preferred_element_type=F32)
    d_scores = probs * (d_probs - jnp.sum(probs * d_probs, axis=2, keepdims=True)) * SCALE
    d_scores = d_scores.astype(BF16)
    d_query = jnp.einsum("rqk,kd->qrd", d_scores, key, preferred_element_type=F32)
    d_query = d_query.reshape(rows, -1).astype(BF16)
    d_key = jnp.einsum("rqk,qrd->kd", d_scores, heads, preferred_element_type=F32).astype(BF16)
    return d_query, d_key, d_value


def norm_back(d_cols, w_query, w_key, w_value, saved):
    d_query, d_key, d_value = d_cols
    d_normed = dot_nt(d_query, w_query) + dot_nt(d_key, w_key) + dot_nt(d_value, w_value)
    wide = saved["full"].astype(F32) * saved["inv_rms"]
    return saved["inv_rms"] * (
        d_normed - wide * jnp.mean(d_normed * wide, axis=1, keepdims=True)
    )


def on_device(embeds, lengths, owners, w_query, w_key, w_value, w_out, cycle_grad):
    pairs = lax.axis_size("dp")
    dp_self = lax.axis_index("dp")
    rows, width = embeds.shape[1:]
    w_query, w_key, w_value, w_out = w_query[0], w_key[0], w_value[0], w_out[0]

    own_len = lax.dynamic_slice_in_dim(lengths, dp_self, 1, 0)[0]
    own_owner = lax.dynamic_slice_in_dim(owners, dp_self, 1, 0)[0]
    slots = jnp.arange(pairs, dtype=jnp.int32)
    ends = jnp.sum(jnp.where(slots[None, :] <= slots[:, None], own_len[None, :], 0), axis=1)
    starts = ends - own_len
    live_ids = jnp.arange(LIVE, dtype=jnp.int32)
    in_slot = (live_ids[:, None] >= starts[None, :]) & (live_ids[:, None] < ends[None, :])

    def of_slot(table):
        return jnp.sum(jnp.where(in_slot, table[None, :], 0), axis=1)

    slot = of_slot(slots)
    place = live_ids - of_slot(starts)
    at_source = slot * SLOT + place
    at_owner = of_slot(own_owner) * SLOT + place
    row_ids = jnp.arange(rows, dtype=jnp.int32)
    from_source = (at_source[:, None] == row_ids[None, :]).astype(BF16)
    from_owner = (at_owner[:, None] == row_ids[None, :]).astype(BF16)
    allowed = (slot[:, None] == slot[None, :]) & (live_ids[None, :] <= live_ids[:, None])

    def regroup(block):
        split = block.reshape(pairs, SLOT, width)
        return lax.all_to_all(split, "dp", split_axis=0, concat_axis=0, tiled=True).reshape(
            rows, width
        )

    barrier = lax.optimization_barrier
    wq, wk = w_query.shape[1], w_key.shape[1]
    grad_rows = regroup(cycle_grad[0])
    moved = dot(from_source, embeds[0]).astype(BF16)
    moved_full = widen(moved)
    first = attend(moved_full, w_query, w_key, w_value, allowed)
    branch = narrow(dot(first["attended"], w_out))
    decoded = (moved.astype(F32) + branch).astype(BF16)
    grad = dot(from_owner, grad_rows).astype(BF16)
    decoded, grad = barrier((decoded, grad))
    incoming = partner(decoded)
    incoming_full, grad = widen(incoming, grad)
    grad_full = widen(grad)
    second = attend(incoming_full, w_query, w_key, w_value, allowed)
    branch = dot(second["attended"], w_out).astype(BF16)
    grad_full, branch = barrier((grad_full, branch))
    cols_second = attend_back(dot_nt(grad_full, w_out).astype(BF16), second)
    branch, cols_second = narrow(branch, cols_second)
    d_second = norm_back(cols_second, w_query, w_key, w_value, second)
    d_second, branch = barrier((d_second, branch))
    cycled = (incoming.astype(F32) + branch).astype(BF16)
    cycled_rows = regroup(dot_tn(from_owner, cycled).astype(BF16))
    back = (grad.astype(F32) + narrow(d_second)).astype(BF16)
    ret = partner(back)
    norm = split_by_core(stack([second["normed"], first["normed"]]))
    att = stack([second["attended"], first["attended"]])
    ret, cycled_rows, norm, att = barrier((ret, cycled_rows, norm, att))
    ret_full = widen(ret)
    left = split_by_core(stack([grad_full, ret_full]))
    out_sum = product_over_core(*left, att)
    d_attended = dot_nt(ret_full, w_out).astype(BF16)
    out_sum, d_attended = barrier((out_sum, d_attended))
    cols_first = attend_back(d_attended, first)
    cols = stack([jnp.concatenate(cols_second, axis=1), jnp.concatenate(cols_first, axis=1)])
    qkv_sum = product_over_core(*norm, cols)
    qkv_sum, cols_first = barrier((qkv_sum, cols_first))
    d_first = norm_back(cols_first, w_query, w_key, w_value, first)
    out_sum, qkv_own, d_first = sum_over_y(out_sum, 1, None, (qkv_sum, d_first))
    qkv_sum = sum_over_y(qkv_sum, 1, qkv_own)
    out_sum = sum_over_z(out_sum, 0)
    qkv_sum = sum_over_z(qkv_sum, 0)
    front = (ret.astype(F32) + narrow(d_first)).astype(BF16)
    restored = dot_tn(from_source, front).astype(BF16)
    return (
        cycled_rows[None],
        restored[None],
        qkv_sum[None, :, :wq],
        qkv_sum[None, :, wq : wq + wk],
        qkv_sum[None, :, wq + wk :],
        out_sum[None],
    )


def solution(mesh):
    rows = P("section", "dp", "mp")
    columns = P("section", None, "mp")
    return jax.shard_map(
        on_device,
        mesh=mesh,
        in_specs=(rows, P(), P(), columns, columns, columns, P("section", "mp", None), rows),
        out_specs=(rows,) * 6,
        check_vma=False,
    )
```

```python
import math

import jax
import jax.numpy as jnp
from jax import lax
from jax.experimental import pallas as pl
from jax.experimental.pallas import tpu as pltpu
from jax.sharding import PartitionSpec as P

HEAD_DIM = 128
SLOT = 6
LIVE = 120
EPS = 1e-05
SCALE = 1.0 / math.sqrt(HEAD_DIM)
F32 = jnp.float32
BF16 = jnp.bfloat16
NT = (((1,), (1,)), ((), ()))
TN = (((0,), (0,)), ((), ()))


def dot(a, b):
    return jnp.dot(a, b, preferred_element_type=F32)


def dot_nt(a, b):
    return lax.dot_general(a, b, NT, preferred_element_type=F32)


def dot_tn(a, b):
    return lax.dot_general(a, b, TN, preferred_element_type=F32)


def shift(block, axis, by):
    count = lax.axis_size(axis)
    return lax.ppermute(block, axis, [(i, (i + by) % count) for i in range(count)])


def widen(shard, behind=None):
    me = lax.axis_index("mp")
    width = shard.shape[1]
    across = shift(shard, "mp", 2)
    right = shift(shard, "mp", 1)
    left = shift(shard, "mp", 3)
    if behind is not None:
        right, behind = lax.optimization_barrier((right, behind))
    full = jnp.zeros((shard.shape[0], 4 * width), shard.dtype)
    for block, by in ((shard, 0), (right, 3), (left, 1), (across, 2)):
        full = lax.dynamic_update_slice(full, block, (0, (me + by) % 4 * width))
    return full if behind is None else (full, behind)


def narrow(partial):
    me = lax.axis_index("mp")
    width = partial.shape[1] // 4

    def block(by):
        return lax.dynamic_slice(
            partial, (0, (me + by) % 4 * width), (partial.shape[0], width)
        )

    across = shift(block(2).astype(BF16), "mp", 2)
    right = shift(block(1).astype(BF16), "mp", 1)
    left = shift(block(3).astype(BF16), "mp", 3)
    return block(0) + right.astype(F32) + left.astype(F32) + across.astype(F32)


def partner(block):
    return lax.ppermute(block, "section", [(0, 1), (1, 0)])


def shift_part(block, stride, size, by):
    count = lax.axis_size("dp")
    route = []
    for i in range(count):
        part = i // stride % size
        route.append((i, i + ((part + by) % size - part) * stride))
    return lax.ppermute(block, "dp", route)


def other_core(block):
    return shift_part(block, 1, 2, 1)


def stack(blocks):
    rows, cols = blocks[0].shape
    held = jnp.zeros((len(blocks) * rows, cols), blocks[0].dtype)
    for k, block in enumerate(blocks):
        held = lax.dynamic_update_slice(held, block, (k * rows, 0))
    return held


def pick(blocks, at, axis):
    return lax.dynamic_index_in_dim(blocks, at, axis, keepdims=False)


def split_kernel(core, a_ref, mine_ref, other_ref):
    for out_ref, which in ((mine_ref, core[0]), (other_ref, 1 - core[0])):
        for j in range(16):
            at = pl.multiple_of((2 * j + which) * 128, 128)
            out_ref[:, j * 128 : (j + 1) * 128] = a_ref[:, pl.ds(at, 128)]


def split_by_core(a):
    rows, cols = a.shape
    half = jax.ShapeDtypeStruct((rows, cols // 2), a.dtype)
    vmem = pl.BlockSpec(memory_space=pltpu.VMEM)
    core = lax.axis_index("dp") % 2
    return pl.pallas_call(
        split_kernel,
        out_shape=(half, half),
        in_specs=[pl.BlockSpec(memory_space=pltpu.SMEM), vmem],
        out_specs=(vmem, vmem),
        cost_estimate=pl.CostEstimate(
            flops=rows * cols, bytes_accessed=4 * rows * cols, transcendentals=0
        ),
        name="split_by_core",
    )(core.reshape(1), a)


def product_over_core(mine, other, right):
    came = other_core(dot_tn(other, right).astype(BF16))
    total = (dot_tn(mine, right) + came.astype(F32)).astype(BF16)
    return total.reshape(4, 4, 128, -1)


def sum_over_four(total, at, stride, axis, own=None, ahead=()):
    came = [
        shift_part(pick(total, (at + by) % 4, axis).astype(BF16), stride, 4, by)
        for by in (2, 1, 3)
    ]
    came, ahead = lax.optimization_barrier((came, ahead))
    held = pick(total if own is None else own, at % 4, axis).astype(F32)
    for block in came:
        held = held + block.astype(F32)
    return (held, *ahead) if ahead else held


def sum_over_y(total, axis, own=None, ahead=()):
    return sum_over_four(total, lax.axis_index("dp") // 2, 2, axis, own, ahead)


def sum_over_z(total, axis):
    return sum_over_four(total, lax.axis_index("dp") // 8, 8, axis)


def attend(full, w_query, w_key, w_value, allowed):
    wide = full.astype(F32)
    inv_rms = lax.rsqrt(jnp.mean(wide * wide, axis=1, keepdims=True) + EPS)
    normed = (wide * inv_rms).astype(BF16)
    query = dot(normed, w_query).astype(BF16)
    key = dot(normed, w_key).astype(BF16)
    value = dot(normed, w_value).astype(BF16)
    heads = query.reshape(query.shape[0], -1, HEAD_DIM)
    scores = jnp.einsum("qrd,kd->rqk", heads, key, preferred_element_type=F32) * SCALE
    raised = jnp.exp(jnp.where(allowed, scores, -jnp.inf))
    probs = raised / jnp.sum(raised, axis=2, keepdims=True)
    probs_low = probs.astype(BF16)
    attended = jnp.einsum("rqk,kd->qrd", probs_low, value, preferred_element_type=F32)
    attended = attended.reshape(query.shape).astype(BF16)
    return dict(
        full=full,
        inv_rms=inv_rms,
        normed=normed,
        heads=heads,
        key=key,
        value=value,
        probs=probs,
        probs_low=probs_low,
        attended=attended,
    )


def attend_back(d_attended, saved):
    rows = d_attended.shape[0]
    probs, key, value, heads = saved["probs"], saved["key"], saved["value"], saved["heads"]
    d_heads = d_attended.reshape(heads.shape)
    d_value = jnp.einsum("rqk,qrd->kd", saved["probs_low"], d_heads, preferred_element_type=F32)
    d_value = d_value.astype(BF16)
    d_probs = jnp.einsum("qrd,kd->rqk", d_heads, value, preferred_element_type=F32)
    d_scores = probs * (d_probs - jnp.sum(probs * d_probs, axis=2, keepdims=True)) * SCALE
    d_scores = d_scores.astype(BF16)
    d_query = jnp.einsum("rqk,kd->qrd", d_scores, key, preferred_element_type=F32)
    d_query = d_query.reshape(rows, -1).astype(BF16)
    d_key = jnp.einsum("rqk,qrd->kd", d_scores, heads, preferred_element_type=F32).astype(BF16)
    return d_query, d_key, d_value


def norm_back(d_cols, w_query, w_key, w_value, saved):
    d_query, d_key, d_value = d_cols
    d_normed = dot_nt(d_query, w_query) + dot_nt(d_key, w_key) + dot_nt(d_value, w_value)
    wide = saved["full"].astype(F32) * saved["inv_rms"]
    return saved["inv_rms"] * (
        d_normed - wide * jnp.mean(d_normed * wide, axis=1, keepdims=True)
    )


def on_device(embeds, lengths, owners, w_query, w_key, w_value, w_out, cycle_grad):
    pairs = lax.axis_size("dp")
    dp_self = lax.axis_index("dp")
    rows, width = embeds.shape[1:]
    w_query, w_key, w_value, w_out = w_query[0], w_key[0], w_value[0], w_out[0]

    own_len = lax.dynamic_slice_in_dim(lengths, dp_self, 1, 0)[0]
    own_owner = lax.dynamic_slice_in_dim(owners, dp_self, 1, 0)[0]
    slots = jnp.arange(pairs, dtype=jnp.int32)
    ends = jnp.sum(jnp.where(slots[None, :] <= slots[:, None], own_len[None, :], 0), axis=1)
    starts = ends - own_len
    live_ids = jnp.arange(LIVE, dtype=jnp.int32)
    in_slot = (live_ids[:, None] >= starts[None, :]) & (live_ids[:, None] < ends[None, :])

    def of_slot(table):
        return jnp.sum(jnp.where(in_slot, table[None, :], 0), axis=1)

    slot = of_slot(slots)
    place = live_ids - of_slot(starts)
    at_source = slot * SLOT + place
    at_owner = of_slot(own_owner) * SLOT + place
    row_ids = jnp.arange(rows, dtype=jnp.int32)
    from_source = (at_source[:, None] == row_ids[None, :]).astype(BF16)
    from_owner = (at_owner[:, None] == row_ids[None, :]).astype(BF16)
    allowed = (slot[:, None] == slot[None, :]) & (live_ids[None, :] <= live_ids[:, None])

    def regroup(block):
        split = block.reshape(pairs, SLOT, width)
        return lax.all_to_all(split, "dp", split_axis=0, concat_axis=0, tiled=True).reshape(
            rows, width
        )

    barrier = lax.optimization_barrier
    wq, wk = w_query.shape[1], w_key.shape[1]
    grad_rows = regroup(cycle_grad[0])
    moved = dot(from_source, embeds[0]).astype(BF16)
    moved_full = widen(moved)
    first = attend(moved_full, w_query, w_key, w_value, allowed)
    branch = narrow(dot(first["attended"], w_out))
    decoded = (moved.astype(F32) + branch).astype(BF16)
    grad = dot(from_owner, grad_rows).astype(BF16)
    decoded, grad = barrier((decoded, grad))
    incoming = partner(decoded)
    incoming_full, grad = widen(incoming, grad)
    grad_full = widen(grad)
    second = attend(incoming_full, w_query, w_key, w_value, allowed)
    branch = dot(second["attended"], w_out).astype(BF16)
    branch = branch.reshape(LIVE, 4, -1).transpose(1, 0, 2)
    grad_full, branch = barrier((grad_full, branch))
    cols_second = attend_back(dot_nt(grad_full, w_out).astype(BF16), second)
    d_second = norm_back(cols_second, w_query, w_key, w_value, second)
    back = (grad.astype(F32) + narrow(d_second)).astype(BF16)
    back, branch = barrier((back, branch))
    ret = partner(back)
    branch = lax.all_to_all(branch, "mp", split_axis=0, concat_axis=0, tiled=True)
    norm = split_by_core(stack([second["normed"], first["normed"]]))
    att = stack([second["attended"], first["attended"]])
    ret, norm, att = barrier((ret, norm, att))
    ret_full, branch = widen(ret, branch)
    cycled = (incoming.astype(F32) + jnp.sum(branch.astype(F32), axis=0)).astype(BF16)
    left = split_by_core(stack([grad_full, ret_full]))
    out_sum = product_over_core(*left, att)
    d_attended = dot_nt(ret_full, w_out).astype(BF16)
    out_sum, d_attended = barrier((out_sum, d_attended))
    cols_first = attend_back(d_attended, first)
    cols = stack([jnp.concatenate(cols_second, axis=1), jnp.concatenate(cols_first, axis=1)])
    qkv_sum = product_over_core(*norm, cols)
    qkv_sum, cols_first = barrier((qkv_sum, cols_first))
    d_first = norm_back(cols_first, w_query, w_key, w_value, first)
    out_sum, qkv_own, d_first, cycled = sum_over_y(
        out_sum, 1, None, (qkv_sum, d_first, cycled)
    )
    cycled_rows = regroup(dot_tn(from_owner, cycled).astype(BF16))
    qkv_sum, cycled_rows = sum_over_y(qkv_sum, 1, qkv_own, (cycled_rows,))
    out_sum = sum_over_z(out_sum, 0)
    qkv_sum = sum_over_z(qkv_sum, 0)
    front = (ret.astype(F32) + narrow(d_first)).astype(BF16)
    restored = dot_tn(from_source, front).astype(BF16)
    return (
        cycled_rows[None],
        restored[None],
        qkv_sum[None, :, :wq],
        qkv_sum[None, :, wq : wq + wk],
        qkv_sum[None, :, wq + wk :],
        out_sum[None],
    )


def solution(mesh):
    rows = P("section", "dp", "mp")
    columns = P("section", None, "mp")
    return jax.shard_map(
        on_device,
        mesh=mesh,
        in_specs=(rows, P(), P(), columns, columns, columns, P("section", "mp", None), rows),
        out_specs=(rows,) * 6,
        check_vma=False,
    )
```

```python
import math

import jax
import jax.numpy as jnp
from jax import lax
from jax.experimental import pallas as pl
from jax.experimental.pallas import tpu as pltpu
from jax.sharding import PartitionSpec as P

HEAD_DIM = 128
SLOT = 6
LIVE = 120
EPS = 1e-05
SCALE = 1.0 / math.sqrt(HEAD_DIM)
F32 = jnp.float32
BF16 = jnp.bfloat16
NT = (((1,), (1,)), ((), ()))
TN = (((0,), (0,)), ((), ()))


def dot(a, b):
    return jnp.dot(a, b, preferred_element_type=F32)


def dot_nt(a, b):
    return lax.dot_general(a, b, NT, preferred_element_type=F32)


def dot_tn(a, b):
    return lax.dot_general(a, b, TN, preferred_element_type=F32)


def shift(block, axis, by):
    count = lax.axis_size(axis)
    return lax.ppermute(block, axis, [(i, (i + by) % count) for i in range(count)])


def widen(shard, behind=None):
    me = lax.axis_index("mp")
    width = shard.shape[1]
    across = shift(shard, "mp", 2)
    right = shift(shard, "mp", 1)
    left = shift(shard, "mp", 3)
    if behind is not None:
        right, behind = lax.optimization_barrier((right, behind))
    full = jnp.zeros((shard.shape[0], 4 * width), shard.dtype)
    for block, by in ((shard, 0), (right, 3), (left, 1), (across, 2)):
        full = lax.dynamic_update_slice(full, block, (0, (me + by) % 4 * width))
    return full if behind is None else (full, behind)


def narrow(partial):
    me = lax.axis_index("mp")
    width = partial.shape[1] // 4

    def block(by):
        return lax.dynamic_slice(
            partial, (0, (me + by) % 4 * width), (partial.shape[0], width)
        )

    across = shift(block(2).astype(BF16), "mp", 2)
    right = shift(block(1).astype(BF16), "mp", 1)
    left = shift(block(3).astype(BF16), "mp", 3)
    return block(0) + right.astype(F32) + left.astype(F32) + across.astype(F32)


def partner(block):
    return lax.ppermute(block, "section", [(0, 1), (1, 0)])


def shift_part(block, stride, size, by):
    count = lax.axis_size("dp")
    route = []
    for i in range(count):
        part = i // stride % size
        route.append((i, i + ((part + by) % size - part) * stride))
    return lax.ppermute(block, "dp", route)


def other_core(block):
    return shift_part(block, 1, 2, 1)


def stack(blocks):
    rows, cols = blocks[0].shape
    held = jnp.zeros((len(blocks) * rows, cols), blocks[0].dtype)
    for k, block in enumerate(blocks):
        held = lax.dynamic_update_slice(held, block, (k * rows, 0))
    return held


def pick(blocks, at, axis):
    return lax.dynamic_index_in_dim(blocks, at, axis, keepdims=False)


def split_kernel(core, a_ref, mine_ref, other_ref):
    for out_ref, which in ((mine_ref, core[0]), (other_ref, 1 - core[0])):
        for j in range(16):
            at = pl.multiple_of((2 * j + which) * 128, 128)
            out_ref[:, j * 128 : (j + 1) * 128] = a_ref[:, pl.ds(at, 128)]


def split_by_core(a):
    rows, cols = a.shape
    half = jax.ShapeDtypeStruct((rows, cols // 2), a.dtype)
    vmem = pl.BlockSpec(memory_space=pltpu.VMEM)
    core = lax.axis_index("dp") % 2
    return pl.pallas_call(
        split_kernel,
        out_shape=(half, half),
        in_specs=[pl.BlockSpec(memory_space=pltpu.SMEM), vmem],
        out_specs=(vmem, vmem),
        cost_estimate=pl.CostEstimate(
            flops=rows * cols, bytes_accessed=4 * rows * cols, transcendentals=0
        ),
        name="split_by_core",
    )(core.reshape(1), a)


def product_over_core(mine, other, right):
    came = other_core(dot_tn(other, right).astype(BF16))
    total = (dot_tn(mine, right) + came.astype(F32)).astype(BF16)
    return total.reshape(4, 4, 128, -1)


def sum_over_four(total, at, stride, axis, own=None, ahead=()):
    came = [
        shift_part(pick(total, (at + by) % 4, axis).astype(BF16), stride, 4, by)
        for by in (2, 1, 3)
    ]
    came, ahead = lax.optimization_barrier((came, ahead))
    held = pick(total if own is None else own, at % 4, axis).astype(F32)
    for block in came:
        held = held + block.astype(F32)
    return (held, *ahead) if ahead else held


def sum_over_y(total, axis, own=None, ahead=()):
    return sum_over_four(total, lax.axis_index("dp") // 2, 2, axis, own, ahead)


def sum_over_z(total, axis, ahead=()):
    return sum_over_four(total, lax.axis_index("dp") // 8, 8, axis, None, ahead)


def attend(full, w_query, w_key, w_value, allowed):
    wide = full.astype(F32)
    inv_rms = lax.rsqrt(jnp.mean(wide * wide, axis=1, keepdims=True) + EPS)
    normed = (wide * inv_rms).astype(BF16)
    query = dot(normed, w_query).astype(BF16)
    key = dot(normed, w_key).astype(BF16)
    value = dot(normed, w_value).astype(BF16)
    heads = query.reshape(query.shape[0], -1, HEAD_DIM)
    scores = jnp.einsum("qrd,kd->rqk", heads, key, preferred_element_type=F32) * SCALE
    raised = jnp.exp(jnp.where(allowed, scores, -jnp.inf))
    probs = raised / jnp.sum(raised, axis=2, keepdims=True)
    probs_low = probs.astype(BF16)
    attended = jnp.einsum("rqk,kd->qrd", probs_low, value, preferred_element_type=F32)
    attended = attended.reshape(query.shape).astype(BF16)
    return dict(
        full=full,
        inv_rms=inv_rms,
        normed=normed,
        heads=heads,
        key=key,
        value=value,
        probs=probs,
        probs_low=probs_low,
        attended=attended,
    )


def attend_back(d_attended, saved):
    rows = d_attended.shape[0]
    probs, key, value, heads = saved["probs"], saved["key"], saved["value"], saved["heads"]
    d_heads = d_attended.reshape(heads.shape)
    d_value = jnp.einsum("rqk,qrd->kd", saved["probs_low"], d_heads, preferred_element_type=F32)
    d_value = d_value.astype(BF16)
    d_probs = jnp.einsum("qrd,kd->rqk", d_heads, value, preferred_element_type=F32)
    d_scores = probs * (d_probs - jnp.sum(probs * d_probs, axis=2, keepdims=True)) * SCALE
    d_scores = d_scores.astype(BF16)
    d_query = jnp.einsum("rqk,kd->qrd", d_scores, key, preferred_element_type=F32)
    d_query = d_query.reshape(rows, -1).astype(BF16)
    d_key = jnp.einsum("rqk,qrd->kd", d_scores, heads, preferred_element_type=F32).astype(BF16)
    return d_query, d_key, d_value


def norm_back(d_cols, w_query, w_key, w_value, saved):
    d_query, d_key, d_value = d_cols
    d_normed = dot_nt(d_query, w_query) + dot_nt(d_key, w_key) + dot_nt(d_value, w_value)
    wide = saved["full"].astype(F32) * saved["inv_rms"]
    return saved["inv_rms"] * (
        d_normed - wide * jnp.mean(d_normed * wide, axis=1, keepdims=True)
    )


def on_device(embeds, lengths, owners, w_query, w_key, w_value, w_out, cycle_grad):
    pairs = lax.axis_size("dp")
    dp_self = lax.axis_index("dp")
    rows, width = embeds.shape[1:]
    w_query, w_key, w_value, w_out = w_query[0], w_key[0], w_value[0], w_out[0]

    own_len = lax.dynamic_slice_in_dim(lengths, dp_self, 1, 0)[0]
    own_owner = lax.dynamic_slice_in_dim(owners, dp_self, 1, 0)[0]
    slots = jnp.arange(pairs, dtype=jnp.int32)
    ends = jnp.sum(jnp.where(slots[None, :] <= slots[:, None], own_len[None, :], 0), axis=1)
    starts = ends - own_len
    live_ids = jnp.arange(LIVE, dtype=jnp.int32)
    in_slot = (live_ids[:, None] >= starts[None, :]) & (live_ids[:, None] < ends[None, :])

    def of_slot(table):
        return jnp.sum(jnp.where(in_slot, table[None, :], 0), axis=1)

    slot = of_slot(slots)
    place = live_ids - of_slot(starts)
    at_source = slot * SLOT + place
    at_owner = of_slot(own_owner) * SLOT + place
    row_ids = jnp.arange(rows, dtype=jnp.int32)
    from_source = (at_source[:, None] == row_ids[None, :]).astype(BF16)
    from_owner = (at_owner[:, None] == row_ids[None, :]).astype(BF16)
    allowed = (slot[:, None] == slot[None, :]) & (live_ids[None, :] <= live_ids[:, None])

    def regroup(block):
        split = block.reshape(pairs, SLOT, width)
        return lax.all_to_all(split, "dp", split_axis=0, concat_axis=0, tiled=True).reshape(
            rows, width
        )

    barrier = lax.optimization_barrier
    wq, wk = w_query.shape[1], w_key.shape[1]
    grad_rows = regroup(cycle_grad[0])
    moved = dot(from_source, embeds[0]).astype(BF16)
    moved_full = widen(moved)
    first = attend(moved_full, w_query, w_key, w_value, allowed)
    branch = narrow(dot(first["attended"], w_out))
    decoded = (moved.astype(F32) + branch).astype(BF16)
    grad = dot(from_owner, grad_rows).astype(BF16)
    decoded, grad = barrier((decoded, grad))
    incoming = partner(decoded)
    incoming_full, grad = widen(incoming, grad)
    grad_full = widen(grad)
    second = attend(incoming_full, w_query, w_key, w_value, allowed)
    branch = dot(second["attended"], w_out).astype(BF16)
    branch = branch.reshape(LIVE, 4, -1).transpose(1, 0, 2)
    grad_full, branch = barrier((grad_full, branch))
    cols_second = attend_back(dot_nt(grad_full, w_out).astype(BF16), second)
    d_second = norm_back(cols_second, w_query, w_key, w_value, second)
    back = (grad.astype(F32) + narrow(d_second)).astype(BF16)
    back, branch = barrier((back, branch))
    ret = partner(back)
    branch = lax.all_to_all(branch, "mp", split_axis=0, concat_axis=0, tiled=True)
    norm = split_by_core(stack([second["normed"], first["normed"]]))
    att = stack([second["attended"], first["attended"]])
    ret, norm, att = barrier((ret, norm, att))
    ret_full, branch = widen(ret, branch)
    left = split_by_core(stack([grad_full, ret_full]))
    out_sum = product_over_core(*left, att)
    d_attended = dot_nt(ret_full, w_out).astype(BF16)
    out_sum, d_attended = barrier((out_sum, d_attended))
    cols_first = attend_back(d_attended, first)
    cols = stack([jnp.concatenate(cols_second, axis=1), jnp.concatenate(cols_first, axis=1)])
    qkv_sum = product_over_core(*norm, cols)
    qkv_sum, cols_first = barrier((qkv_sum, cols_first))
    d_first = norm_back(cols_first, w_query, w_key, w_value, first)
    out_sum, qkv_own, d_first = sum_over_y(out_sum, 1, None, (qkv_sum, d_first))
    out_sum, branch = sum_over_z(out_sum, 0, (branch,))
    cycled = (incoming.astype(F32) + jnp.sum(branch.astype(F32), axis=0)).astype(BF16)
    cycled_rows = regroup(dot_tn(from_owner, cycled).astype(BF16))
    qkv_sum = sum_over_y(qkv_sum, 1, qkv_own)
    qkv_sum, cycled_rows = sum_over_z(qkv_sum, 0, (cycled_rows,))
    front = (ret.astype(F32) + narrow(d_first)).astype(BF16)
    restored = dot_tn(from_source, front).astype(BF16)
    return (
        cycled_rows[None],
        restored[None],
        qkv_sum[None, :, :wq],
        qkv_sum[None, :, wq : wq + wk],
        qkv_sum[None, :, wq + wk :],
        out_sum[None],
    )


def solution(mesh):
    rows = P("section", "dp", "mp")
    columns = P("section", None, "mp")
    return jax.shard_map(
        on_device,
        mesh=mesh,
        in_specs=(rows, P(), P(), columns, columns, columns, P("section", "mp", None), rows),
        out_specs=(rows,) * 6,
        check_vma=False,
    )
```

```python
import math

import jax
import jax.numpy as jnp
from jax import lax
from jax.experimental import pallas as pl
from jax.experimental.pallas import tpu as pltpu
from jax.sharding import PartitionSpec as P

HEAD_DIM = 128
SLOT = 6
LIVE = 120
EPS = 1e-05
SCALE = 1.0 / math.sqrt(HEAD_DIM)
F32 = jnp.float32
BF16 = jnp.bfloat16
NT = (((1,), (1,)), ((), ()))
TN = (((0,), (0,)), ((), ()))


def dot(a, b):
    return jnp.dot(a, b, preferred_element_type=F32)


def dot_nt(a, b):
    return lax.dot_general(a, b, NT, preferred_element_type=F32)


def dot_tn(a, b):
    return lax.dot_general(a, b, TN, preferred_element_type=F32)


def shift(block, axis, by):
    count = lax.axis_size(axis)
    return lax.ppermute(block, axis, [(i, (i + by) % count) for i in range(count)])


def widen(shard, behind=None):
    me = lax.axis_index("mp")
    width = shard.shape[1]
    across = shift(shard, "mp", 2)
    right = shift(shard, "mp", 1)
    left = shift(shard, "mp", 3)
    if behind is not None:
        right, behind = lax.optimization_barrier((right, behind))
    full = jnp.zeros((shard.shape[0], 4 * width), shard.dtype)
    for block, by in ((shard, 0), (right, 3), (left, 1), (across, 2)):
        full = lax.dynamic_update_slice(full, block, (0, (me + by) % 4 * width))
    return full if behind is None else (full, behind)


def narrow(partial):
    me = lax.axis_index("mp")
    width = partial.shape[1] // 4

    def block(by):
        return lax.dynamic_slice(
            partial, (0, (me + by) % 4 * width), (partial.shape[0], width)
        )

    across = shift(block(2).astype(BF16), "mp", 2)
    right = shift(block(1).astype(BF16), "mp", 1)
    left = shift(block(3).astype(BF16), "mp", 3)
    return block(0) + right.astype(F32) + left.astype(F32) + across.astype(F32)


def partner(block):
    return lax.ppermute(block, "section", [(0, 1), (1, 0)])


def shift_part(block, stride, size, by):
    count = lax.axis_size("dp")
    route = []
    for i in range(count):
        part = i // stride % size
        route.append((i, i + ((part + by) % size - part) * stride))
    return lax.ppermute(block, "dp", route)


def other_core(block):
    return shift_part(block, 1, 2, 1)


def stack(blocks):
    rows, cols = blocks[0].shape
    held = jnp.zeros((len(blocks) * rows, cols), blocks[0].dtype)
    for k, block in enumerate(blocks):
        held = lax.dynamic_update_slice(held, block, (k * rows, 0))
    return held


def pick(blocks, at, axis):
    return lax.dynamic_index_in_dim(blocks, at, axis, keepdims=False)


def split_kernel(core, a_ref, mine_ref, other_ref):
    for out_ref, which in ((mine_ref, core[0]), (other_ref, 1 - core[0])):
        for j in range(16):
            at = pl.multiple_of((2 * j + which) * 128, 128)
            out_ref[:, j * 128 : (j + 1) * 128] = a_ref[:, pl.ds(at, 128)]


def split_by_core(a):
    rows, cols = a.shape
    half = jax.ShapeDtypeStruct((rows, cols // 2), a.dtype)
    vmem = pl.BlockSpec(memory_space=pltpu.VMEM)
    core = lax.axis_index("dp") % 2
    return pl.pallas_call(
        split_kernel,
        out_shape=(half, half),
        in_specs=[pl.BlockSpec(memory_space=pltpu.SMEM), vmem],
        out_specs=(vmem, vmem),
        cost_estimate=pl.CostEstimate(
            flops=rows * cols, bytes_accessed=4 * rows * cols, transcendentals=0
        ),
        name="split_by_core",
    )(core.reshape(1), a)


def product_over_core(mine, other, right):
    came = other_core(dot_tn(other, right).astype(BF16))
    total = (dot_tn(mine, right) + came.astype(F32)).astype(BF16)
    return total.reshape(4, 4, 128, -1)


def sum_over_four(total, at, stride, axis, own=None, ahead=()):
    came = [
        shift_part(pick(total, (at + by) % 4, axis).astype(BF16), stride, 4, by)
        for by in (2, 1, 3)
    ]
    came, ahead = lax.optimization_barrier((came, ahead))
    held = pick(total if own is None else own, at % 4, axis).astype(F32)
    for block in came:
        held = held + block.astype(F32)
    return (held, *ahead) if ahead else held


def sum_over_y(total, axis, own=None, ahead=()):
    return sum_over_four(total, lax.axis_index("dp") // 2, 2, axis, own, ahead)


def sum_over_z(total, axis, ahead=()):
    return sum_over_four(total, lax.axis_index("dp") // 8, 8, axis, None, ahead)


def attend(full, w_query, w_key, w_value, allowed):
    wide = full.astype(F32)
    inv_rms = lax.rsqrt(jnp.mean(wide * wide, axis=1, keepdims=True) + EPS)
    normed = (wide * inv_rms).astype(BF16)
    query = dot(normed, w_query).astype(BF16)
    key = dot(normed, w_key).astype(BF16)
    value = dot(normed, w_value).astype(BF16)
    heads = query.reshape(query.shape[0], -1, HEAD_DIM)
    scores = jnp.einsum("qrd,kd->rqk", heads, key, preferred_element_type=F32) * SCALE
    raised = jnp.exp(jnp.where(allowed, scores, -jnp.inf))
    probs = raised / jnp.sum(raised, axis=2, keepdims=True)
    probs_low = probs.astype(BF16)
    attended = jnp.einsum("rqk,kd->qrd", probs_low, value, preferred_element_type=F32)
    attended = attended.reshape(query.shape).astype(BF16)
    return dict(
        full=full,
        inv_rms=inv_rms,
        normed=normed,
        heads=heads,
        key=key,
        value=value,
        probs=probs,
        probs_low=probs_low,
        attended=attended,
    )


def attend_back(d_attended, saved):
    rows = d_attended.shape[0]
    probs, key, value, heads = saved["probs"], saved["key"], saved["value"], saved["heads"]
    d_heads = d_attended.reshape(heads.shape)
    d_value = jnp.einsum("rqk,qrd->kd", saved["probs_low"], d_heads, preferred_element_type=F32)
    d_value = d_value.astype(BF16)
    d_probs = jnp.einsum("qrd,kd->rqk", d_heads, value, preferred_element_type=F32)
    d_scores = probs * (d_probs - jnp.sum(probs * d_probs, axis=2, keepdims=True)) * SCALE
    d_scores = d_scores.astype(BF16)
    d_query = jnp.einsum("rqk,kd->qrd", d_scores, key, preferred_element_type=F32)
    d_query = d_query.reshape(rows, -1).astype(BF16)
    d_key = jnp.einsum("rqk,qrd->kd", d_scores, heads, preferred_element_type=F32).astype(BF16)
    return d_query, d_key, d_value


def norm_back(d_cols, w_query, w_key, w_value, saved):
    d_query, d_key, d_value = d_cols
    d_normed = dot_nt(d_query, w_query) + dot_nt(d_key, w_key) + dot_nt(d_value, w_value)
    wide = saved["full"].astype(F32) * saved["inv_rms"]
    return saved["inv_rms"] * (
        d_normed - wide * jnp.mean(d_normed * wide, axis=1, keepdims=True)
    )


def on_device(embeds, lengths, owners, w_query, w_key, w_value, w_out, cycle_grad):
    pairs = lax.axis_size("dp")
    dp_self = lax.axis_index("dp")
    rows, width = embeds.shape[1:]
    w_query, w_key, w_value, w_out = w_query[0], w_key[0], w_value[0], w_out[0]

    own_len = lax.dynamic_slice_in_dim(lengths, dp_self, 1, 0)[0]
    own_owner = lax.dynamic_slice_in_dim(owners, dp_self, 1, 0)[0]
    slots = jnp.arange(pairs, dtype=jnp.int32)
    ends = jnp.sum(jnp.where(slots[None, :] <= slots[:, None], own_len[None, :], 0), axis=1)
    starts = ends - own_len
    live_ids = jnp.arange(LIVE, dtype=jnp.int32)
    in_slot = (live_ids[:, None] >= starts[None, :]) & (live_ids[:, None] < ends[None, :])

    def of_slot(table):
        return jnp.sum(jnp.where(in_slot, table[None, :], 0), axis=1)

    slot = of_slot(slots)
    place = live_ids - of_slot(starts)
    at_source = slot * SLOT + place
    at_owner = of_slot(own_owner) * SLOT + place
    row_ids = jnp.arange(rows, dtype=jnp.int32)
    from_source = (at_source[:, None] == row_ids[None, :]).astype(BF16)
    from_owner = (at_owner[:, None] == row_ids[None, :]).astype(BF16)
    allowed = (slot[:, None] == slot[None, :]) & (live_ids[None, :] <= live_ids[:, None])

    def regroup(block):
        split = block.reshape(pairs, SLOT, width)
        return lax.all_to_all(split, "dp", split_axis=0, concat_axis=0, tiled=True).reshape(
            rows, width
        )

    barrier = lax.optimization_barrier
    wq, wk = w_query.shape[1], w_key.shape[1]
    grad_rows = regroup(cycle_grad[0])
    moved = dot(from_source, embeds[0]).astype(BF16)
    moved_full = widen(moved)
    first = attend(moved_full, w_query, w_key, w_value, allowed)
    branch = narrow(dot(first["attended"], w_out))
    decoded = (moved.astype(F32) + branch).astype(BF16)
    grad = dot(from_owner, grad_rows).astype(BF16)
    decoded, grad = barrier((decoded, grad))
    incoming = partner(decoded)
    incoming_full, grad = widen(incoming, grad)
    grad_full = widen(grad)
    second = attend(incoming_full, w_query, w_key, w_value, allowed)
    branch = dot(second["attended"], w_out).astype(BF16)
    branch = branch.reshape(LIVE, 4, -1).transpose(1, 0, 2)
    grad_full, branch = barrier((grad_full, branch))
    cols_second = attend_back(dot_nt(grad_full, w_out).astype(BF16), second)
    d_second = norm_back(cols_second, w_query, w_key, w_value, second)
    back = (grad.astype(F32) + narrow(d_second)).astype(BF16)
    back, branch = barrier((back, branch))
    ret = partner(back)
    branch = lax.all_to_all(branch, "mp", split_axis=0, concat_axis=0, tiled=True)
    norm = split_by_core(stack([second["normed"], first["normed"]]))
    att = stack([second["attended"], first["attended"]])
    ret, norm, att = barrier((ret, norm, att))
    ret_full, branch = widen(ret, branch)
    left = split_by_core(stack([grad_full, ret_full]))
    out_sum = product_over_core(*left, att)
    d_attended = dot_nt(ret_full, w_out).astype(BF16)
    out_sum, d_attended = barrier((out_sum, d_attended))
    cols_first = attend_back(d_attended, first)
    cols = stack([jnp.concatenate(cols_second, axis=1), jnp.concatenate(cols_first, axis=1)])
    qkv_sum = product_over_core(*norm, cols)
    qkv_sum, cols_first = barrier((qkv_sum, cols_first))
    d_first = norm_back(cols_first, w_query, w_key, w_value, first)
    out_sum, qkv_own = sum_over_y(out_sum, 1, None, (qkv_sum,))
    out_sum, branch = sum_over_z(out_sum, 0, (branch,))
    cycled = (incoming.astype(F32) + jnp.sum(branch.astype(F32), axis=0)).astype(BF16)
    cycled_rows = regroup(dot_tn(from_owner, cycled).astype(BF16))
    qkv_sum = sum_over_y(qkv_sum, 1, qkv_own)
    qkv_sum, cycled_rows = sum_over_z(qkv_sum, 0, (cycled_rows,))
    front = (ret.astype(F32) + narrow(d_first)).astype(BF16)
    restored = dot_tn(from_source, front).astype(BF16)
    return (
        cycled_rows[None],
        restored[None],
        qkv_sum[None, :, :wq],
        qkv_sum[None, :, wq : wq + wk],
        qkv_sum[None, :, wq + wk :],
        out_sum[None],
    )


def solution(mesh):
    rows = P("section", "dp", "mp")
    columns = P("section", None, "mp")
    return jax.shard_map(
        on_device,
        mesh=mesh,
        in_specs=(rows, P(), P(), columns, columns, columns, P("section", "mp", None), rows),
        out_specs=(rows,) * 6,
        check_vma=False,
    )
```
